32 devices in a mesh: seq: 16 (over z, y, x), head: 2 (over core).
Axes of the slice: x: 2, y: 2, z: 4, core: 2. Of those that a mesh axis runs over, the one named last changes fastest.
Arguments:
- attn_q: bfloat16 [2048, 512], P('seq', 'head'), may hold values from -6 to 6
- attn_k: bfloat16 [2048, 512], P('seq', 'head'), may hold values from -6 to 6
- attn_v: bfloat16 [2048, 512], P('seq', 'head'), may hold values from -6 to 6
- attn_out: bfloat16 [2048, 512], P('seq', 'head'), may hold values from -0.29882812 to 0.29882812
- attn_dout: bfloat16 [2048, 512], P('seq', 'head'), may hold values from -96 to 96
- attn_lse: float32 [4, 2048], P('head', 'seq'), may hold values from 7 to 8
- w_kv: bfloat16 [512, 2, 512], P('seq', None, 'head'), may hold values from -0.25 to 0.25
- gdn_q: bfloat16 [2048, 512], P('seq', 'head'), may hold values from -6 to 6
- gdn_k: bfloat16 [2048, 512], P('seq', 'head'), may hold values from -6 to 6
- gdn_v: bfloat16 [2048, 512], P('seq', 'head'), may hold values from -6 to 6
- gdn_dout: bfloat16 [2048, 512], P('seq', 'head'), may hold values from -6 to 6
- gdn_log_decay: float32 [4, 2048], P('head', 'seq'), may hold values from -0.56 to 0
- gdn_beta: float32 [4, 2048], P('head', 'seq'), may hold values from 0 to 0.9
- gdn_states: float32 [32, 4, 128, 128], P('seq', 'head'), may hold values from -24 to 24
Outputs:
- attn_dq: bfloat16 [2048, 512], P('seq', 'head')
- attn_dx: bfloat16 [512, 2048], P('head', 'seq')
- gdn_dq: bfloat16 [2048, 512], P('seq', 'head')
- gdn_dk: bfloat16 [2048, 512], P('seq', 'head')
- gdn_dv: bfloat16 [2048, 512], P('seq', 'head')
- gdn_dlog_decay: float32 [4, 2048], P('head', 'seq')
- gdn_dbeta: float32 [4, 2048], P('head', 'seq')
The draws below stay inside these ranges and needn't reach their ends.
All inputs are finite; a program needn't handle non-finite values.
Results may differ from the reference program's by a relative error of at most 0.0078.
Values may be sent and summed in bfloat16 or wider, within the bound.
A program may use at most 64 MiB of HBM per device.

```python
import math
import jax
import jax.numpy as jnp
from jax import lax

TOK_DEV = 128
HEAD_DIM = 128
BLOCK = 64
WINDOW = 1024
HEADS = 4
WIDTH = 512
TOKENS = 2048
BLOCKS = 32


def head_speed(key):
    share = 0.5
    return jax.random.uniform(jax.random.fold_in(key, 11), (HEADS,)) < share


def draw_gdn_log_decay(key, part):
    lasting = head_speed(key)
    branch = jax.random.fold_in(key, 23)
    key_jitter, key_places, key_losses = jax.random.split(branch, 3)
    speeds = jnp.where(lasting, 0.5 / TOKENS, 1.0 / 48.0)
    jitter = jnp.exp(jax.random.uniform(key_jitter, (HEADS, TOKENS), minval=math.log(0.5), maxval=math.log(2.0)))
    places = jax.random.randint(key_places, (3,), 0, TOKENS)
    positions = jnp.arange(TOKENS)
    struck = jnp.any(positions[:, None] == places[None, :], axis=1)
    losses = jax.random.uniform(key_losses, (HEADS, TOKENS), minval=math.log(0.6), maxval=math.log(0.8))
    return -speeds[:, None] * jitter + jnp.where(struck[None, :], losses, 0.0)


def draw_gdn_beta(key, part):
    lasting = head_speed(key)
    branch = jax.random.fold_in(key, 37)
    key_slow, key_fast = jax.random.split(branch, 2)
    slow_values = jax.random.uniform(key_slow, (HEADS, TOKENS), minval=0.1, maxval=0.3) * (HEAD_DIM / TOKENS)
    fast_values = jax.random.uniform(key_fast, (HEADS, TOKENS), minval=0.3, maxval=0.9)
    return jnp.where(lasting[:, None], slow_values, fast_values)


def block_scale(stream_key, shape, pieces, low, top_value):
    loudness = 1.0
    for position, blocks in pieces:
        steps = jax.random.uniform(jax.random.fold_in(jax.random.fold_in(stream_key, 6), position), (blocks,), jnp.float32, low / len(pieces), top_value / len(pieces))
        loudness = loudness * jnp.repeat(jnp.exp(steps), shape[position] // blocks).reshape((-1,) + (1,) * (len(shape) - 1 - position))
    return loudness


def bell_draw(key, extent, spread, reach, cuts=(), kind=jnp.bfloat16):
    drawn = spread * jax.random.normal(key, extent, jnp.float32)
    if cuts:
        drawn = drawn * block_scale(key, extent, cuts, -0.22, 0.18)
    return jnp.clip(drawn, -reach, reach).astype(kind)


def setup_inputs(seed: int = 0) -> dict:
    streams_of = jax.random.split(jax.random.key(seed), 15)
    return {
        "attn_q": bell_draw(streams_of[0], (TOKENS, WIDTH), 1.0, 6.0, ((0, 16), (1, 2))),
        "attn_k": bell_draw(streams_of[1], (TOKENS, WIDTH), 1.0, 6.0, ((0, 16), (1, 2))),
        "attn_v": bell_draw(streams_of[2], (TOKENS, WIDTH), 1.0, 6.0, ((0, 16), (1, 2))),
        "attn_out": bell_draw(streams_of[3], (TOKENS, WIDTH), 0.05, 0.29882812, ((0, 16), (1, 2))),
        "attn_dout": bell_draw(streams_of[4], (TOKENS, WIDTH), 16.0, 96.0, ((0, 16), (1, 2))),
        "attn_lse": jnp.clip(7.0 + 1.0 * jax.random.uniform(streams_of[5], (HEADS, TOKENS), jnp.float32) ** block_scale(streams_of[5], (HEADS, TOKENS), ((0, 2), (1, 16)), -0.2, 0.2), 7.0, 8.0),
        "w_kv": bell_draw(streams_of[6], (WIDTH, 2, WIDTH), WIDTH ** -0.5, 0.25, ((0, 16), (2, 2))),
        "gdn_q": bell_draw(streams_of[7], (TOKENS, WIDTH), 1.0, 6.0, ((0, 16), (1, 2))),
        "gdn_k": bell_draw(streams_of[8], (TOKENS, WIDTH), 1.0, 6.0, ((0, 16), (1, 2))),
        "gdn_v": bell_draw(streams_of[9], (TOKENS, WIDTH), 1.0, 6.0, ((0, 16), (1, 2))),
        "gdn_dout": bell_draw(streams_of[10], (TOKENS, WIDTH), 1.0, 6.0, ((0, 16), (1, 2))),
        "gdn_log_decay": draw_gdn_log_decay(jax.random.fold_in(streams_of[14], 71), 0),
        "gdn_beta": draw_gdn_beta(jax.random.fold_in(streams_of[14], 71), 0),
        "gdn_states": bell_draw(streams_of[13], (BLOCKS, HEADS, HEAD_DIM, HEAD_DIM), 4.0, 24.0, ((0, 16), (1, 2)), jnp.float32),
    }


HIGH = lax.Precision.HIGHEST

def matmul(left_side, right_side):
    return jnp.dot(left_side, right_side, precision=HIGH)

def unit_rows(matrix):
    return matrix * lax.rsqrt(lax.optimization_barrier(jnp.sum(matrix * matrix, axis=-1, keepdims=True)) + 1e-06)

def inverse_unit(lower_part):
    length = lower_part.shape[0]
    identity = jnp.eye(length, dtype=jnp.float32)
    powered = lower_part
    result = identity - lower_part
    for _ in range(length.bit_length() - 2):
        powered = matmul(powered, powered)
        result = matmul(result, identity + powered)
    return result

def block_parts(queries, keys_in, decays, strengths):
    length, depth = queries.shape
    unit_q = unit_rows(queries) * depth ** (-0.5)
    unit_k = unit_rows(keys_in)
    summed = jnp.cumsum(decays)
    row_ids = lax.broadcasted_iota(jnp.int32, (length, length), 0)
    col_ids = lax.broadcasted_iota(jnp.int32, (length, length), 1)
    causal = row_ids >= col_ids
    fading = jnp.where(causal, jnp.exp(jnp.where(causal, summed[:, None] - summed[None, :], 0.0)), 0.0)
    strict = jnp.where(row_ids > col_ids, fading, 0.0)
    lower_part = strengths[:, None] * strict * matmul(unit_k, unit_k.T)
    solved = inverse_unit(lower_part)
    growth = jnp.exp(summed)
    widened = matmul(solved, (strengths * growth)[:, None] * unit_k)
    attention = fading * matmul(unit_q, unit_k.T)
    tailing = jnp.exp(summed[-1] - summed)[:, None] * unit_k
    return (unit_q, solved, growth, widened, attention, tailing)

def block_forward(queries, keys_in, values, decays, strengths, initial):
    unit_q, solved, growth, widened, attention, tailing = block_parts(queries, keys_in, decays, strengths)
    fresh = matmul(solved, strengths[:, None] * values) - matmul(widened, initial)
    output = growth[:, None] * matmul(unit_q, initial) + matmul(attention, fresh)
    final = growth[-1] * initial + matmul(tailing.T, fresh)
    return (output, final)

def block_adjoint(queries, keys_in, decays, strengths, out_grad):
    unit_q, solved, growth, widened, attention, tailing = block_parts(queries, keys_in, decays, strengths)
    depth = queries.shape[1]
    carry_map = growth[-1] * jnp.eye(depth, dtype=jnp.float32) - matmul(widened.T, tailing)
    local_term = matmul((growth[:, None] * unit_q).T, out_grad) - matmul(widened.T, matmul(attention.T, out_grad))
    return (carry_map, local_term)

def block_grads(queries, keys_in, values, decays, strengths, initial, out_grad, later_adjoint):
    _, pullback = jax.vjp(block_forward, queries, keys_in, values, decays, strengths, initial)
    grad_q, grad_k, grad_v, grad_decay, grad_beta, _ = pullback((out_grad, later_adjoint))
    return (grad_q, grad_k, grad_v, grad_decay, grad_beta)

def gdn_head(inputs):
    head_q, head_k, head_v, head_grad, head_decay, head_beta, saved = inputs
    block_count = head_q.shape[0] // BLOCK

    def blocks(matrix):
        return matrix.reshape(block_count, BLOCK, -1)
    queries, keys_in, values, out_grad = (blocks(head_q), blocks(head_k), blocks(head_v), blocks(head_grad))
    decays = head_decay.reshape(block_count, BLOCK)
    strengths = head_beta.reshape(block_count, BLOCK)
    carry_map, local_term = jax.vmap(block_adjoint)(queries, keys_in, decays, strengths, out_grad)

    def backward(carry, couple):
        return (matmul(couple[0], carry) + couple[1], carry)
    nothing = jnp.zeros(saved.shape[1:], jnp.float32)
    _, later_adjoint = lax.scan(backward, nothing, (carry_map, local_term), reverse=True)
    grad_q, grad_k, grad_v, grad_decay, grad_beta = jax.vmap(block_grads)(queries, keys_in, values, decays, strengths, saved, out_grad, later_adjoint)
    depth = head_q.shape[1]
    return (grad_q.reshape(-1, depth), grad_k.reshape(-1, depth), grad_v.reshape(-1, depth), grad_decay.reshape(-1), grad_beta.reshape(-1))

def attention_terms(queries, keys_in, values, out_grad, log_totals, dot_terms, query_pos, key_pos):
    scaling = queries.shape[1] ** (-0.5)
    query_wide = queries.astype(jnp.float32)
    key_wide = keys_in.astype(jnp.float32)
    grad_wide = out_grad.astype(jnp.float32)
    logits = matmul(query_wide, key_wide.T) * scaling
    distance = query_pos[:, None] - key_pos[None, :]
    visible = (distance >= 0) & (distance < WINDOW) & (key_pos[None, :] >= 0)
    chances = jnp.where(visible, jnp.exp(jnp.where(visible, logits - log_totals[:, None], 0.0)), 0.0)
    grad_prob = matmul(grad_wide, values.astype(jnp.float32).T)
    grad_logit = lax.optimization_barrier((chances * (grad_prob - dot_terms[:, None])).astype(jnp.bfloat16)).astype(jnp.float32)
    weights = lax.optimization_barrier(chances.astype(jnp.bfloat16)).astype(jnp.float32)
    grad_q = matmul(grad_logit, key_wide) * scaling
    grad_k = matmul(grad_logit.T, query_wide) * scaling
    grad_v = matmul(weights.T, grad_wide)
    return (grad_q, grad_k, grad_v)

def attention_head(inputs):
    head_q, head_k, head_v, head_out, head_grad, head_log = inputs
    depth = head_q.shape[1]
    dot_terms = lax.optimization_barrier(jnp.sum(head_grad.astype(jnp.float32) * head_out.astype(jnp.float32), axis=1))
    padding = jnp.zeros((WINDOW, depth), jnp.bfloat16)
    padded_k = jnp.concatenate([padding, head_k], axis=0)
    padded_v = jnp.concatenate([padding, head_v], axis=0)

    def one_block(index):
        row_start = (index * TOK_DEV).astype(jnp.int32)
        queries = lax.dynamic_slice_in_dim(head_q, row_start, TOK_DEV, 0)
        out_grad = lax.dynamic_slice_in_dim(head_grad, row_start, TOK_DEV, 0)
        log_totals = lax.dynamic_slice_in_dim(head_log, row_start, TOK_DEV, 0)
        row_terms = lax.dynamic_slice_in_dim(dot_terms, row_start, TOK_DEV, 0)
        keys_in = lax.dynamic_slice_in_dim(padded_k, row_start, WINDOW + TOK_DEV, 0)
        values = lax.dynamic_slice_in_dim(padded_v, row_start, WINDOW + TOK_DEV, 0)
        query_pos = row_start + jnp.arange(TOK_DEV, dtype=jnp.int32)
        key_pos = row_start - WINDOW + jnp.arange(WINDOW + TOK_DEV, dtype=jnp.int32)
        return attention_terms(queries, keys_in, values, out_grad, log_totals, row_terms, query_pos, key_pos)
    grad_q, grad_k, grad_v = lax.map(one_block, jnp.arange(head_q.shape[0] // TOK_DEV, dtype=jnp.int32))
    reach_count = WINDOW // TOK_DEV

    def gather_back(contrib):
        shaped = contrib.reshape(-1, reach_count + 1, TOK_DEV, depth)
        block_count = shaped.shape[0]
        summed = jnp.zeros((block_count + reach_count, TOK_DEV, depth), jnp.float32)
        for index in range(reach_count + 1):
            summed = summed.at[index:index + block_count].add(shaped[:, index])
        return summed[reach_count:].reshape(-1, depth)
    return (grad_q.reshape(-1, depth), gather_back(grad_k), gather_back(grad_v))

def reference(attn_q, attn_k, attn_v, attn_out, attn_dout, attn_lse, w_kv, gdn_q, gdn_k, gdn_v, gdn_dout, gdn_log_decay, gdn_beta, gdn_states):

    def heads_first(matrix):
        return matrix.reshape(matrix.shape[0], HEADS, -1).transpose(1, 0, 2)

    def tokens_first(stacked):
        return stacked.transpose(1, 0, 2).reshape(stacked.shape[1], -1)
    attn_parts = lax.map(attention_head, (heads_first(attn_q), heads_first(attn_k), heads_first(attn_v), heads_first(attn_out), heads_first(attn_dout), attn_lse))
    attn_dq = tokens_first(attn_parts[0]).astype(jnp.bfloat16)
    key_grad = lax.optimization_barrier(tokens_first(attn_parts[1]).astype(jnp.bfloat16)).astype(jnp.float32)
    value_grad = lax.optimization_barrier(tokens_first(attn_parts[2]).astype(jnp.bfloat16)).astype(jnp.float32)
    weights_wide = w_kv.astype(jnp.float32)
    attn_dx = (matmul(weights_wide[:, 0, :], key_grad.T) + matmul(weights_wide[:, 1, :], value_grad.T)).astype(jnp.bfloat16)

    def heads_wide(matrix):
        return heads_first(matrix.astype(jnp.float32))
    gdn_parts = lax.map(gdn_head, (heads_wide(gdn_q), heads_wide(gdn_k), heads_wide(gdn_v), heads_wide(gdn_dout), gdn_log_decay, gdn_beta, gdn_states.transpose(1, 0, 2, 3)))
    gdn_dq = tokens_first(gdn_parts[0]).astype(jnp.bfloat16)
    gdn_dk = tokens_first(gdn_parts[1]).astype(jnp.bfloat16)
    gdn_dv = tokens_first(gdn_parts[2]).astype(jnp.bfloat16)
    return (attn_dq, attn_dx, gdn_dq, gdn_dk, gdn_dv, gdn_parts[3], gdn_parts[4])
```

```python
import functools
import jax
import jax.numpy as jnp
from jax import lax
from jax.experimental import pallas as pl
from jax.experimental.pallas import tpu as pltpu
from jax.sharding import PartitionSpec as P

BLOCK = 64
WINDOW = 1024
EPS = 1e-06
MESH = pl.DeviceIdType.MESH
F32 = jnp.float32
BF16 = jnp.bfloat16

NN = (((1,), (0,)), ((), ()))
NT = (((1,), (1,)), ((), ()))
TN = (((0,), (0,)), ((), ()))


def dot(left, right, dims=NN):
    return lax.dot_general(left, right, dims, preferred_element_type=F32)


def split(matrix):
    high = matrix.astype(BF16)
    return high, (matrix - high.astype(F32)).astype(BF16)


def mm(left, right, dims=NN):
    left_high, left_low = split(left)
    right_high, right_low = split(right)
    return dot(left_high, right_high, dims) + (
        dot(left_high, right_low, dims) + dot(left_low, right_high, dims)
    )


def mm_full(left, right, dims=NN):
    return lax.dot_general(
        left, right, dims, precision=lax.Precision.HIGHEST, preferred_element_type=F32
    )


def row_sum(matrix):
    return jnp.sum(matrix, axis=1, keepdims=True)


def column_sum(matrix):
    return jnp.sum(matrix, axis=0, keepdims=True)


def stack_heads(matrix, heads):
    depth = matrix.shape[1] // heads
    return jnp.concatenate([matrix[:, h * depth : (h + 1) * depth] for h in range(heads)], axis=0)


def group_size(count):
    size = 1
    while size * size < count:
        size *= 2
    return size if count % size == 0 else count


def kernel(
    n,
    head_n,
    q_ref, k_ref, v_ref, out_ref, dout_ref, lse_ref, w_ref,
    gq_ref, gk_ref, gv_ref, gdo_ref, decay_ref, beta_ref, states_ref,
    dq_out, dx_out, gdq_out, gdk_out, gdv_out, gdecay_out, gbeta_out,
    kv_buf, qd_buf, stat_own, stat_buf, w_all, ab_buf, carry_in, carry_out, dx_send, dx_recv,
    dq_acc, dkv_acc, map_buf,
    kv_send, kv_recv, qd_send, qd_recv, st_send, st_recv, w_send, w_recv,
    ab_send, ab_recv, c_send, c_recv, x_send, x_recv,
):
    me = lax.axis_index("seq")
    my_head = lax.axis_index("head")
    rows, columns = q_ref.shape
    heads = lse_ref.shape[0]
    depth = columns // heads
    reach = WINDOW // rows
    blocks = rows // BLOCK
    total = heads * rows
    size = group_size(n)
    groups = n // size
    rank = lax.rem(me, size)
    group = lax.div(me, size)
    first = group * size

    barrier = pltpu.get_barrier_semaphore()
    for j in range(1, n):
        pl.semaphore_signal(
            barrier, inc=1, device_id={"seq": lax.rem(me + j, n)}, device_id_type=MESH
        )
    for j in range(1, head_n):
        pl.semaphore_signal(
            barrier, inc=1, device_id={"head": lax.rem(my_head + j, head_n)}, device_id_type=MESH
        )

    ones = jnp.ones((8, depth), F32)
    for h in range(heads):
        cols = slice(h * depth, (h + 1) * depth)
        product = dout_ref[:, cols].astype(F32) * out_ref[:, cols].astype(F32)
        stat_own[h : h + 1, :] = lse_ref[h : h + 1, :]
        stat_own[heads + h : heads + h + 1, :] = mm_full(ones, product, NT)[0:1, :]
    pl.semaphore_wait(barrier, n - 1 + head_n - 1)

    def kv_copy(j, which):
        return pltpu.make_async_remote_copy(
            src_ref=(k_ref, v_ref)[which],
            dst_ref=kv_buf.at[j - 1, which],
            send_sem=kv_send.at[j - 1, which],
            recv_sem=kv_recv.at[j - 1, which],
            device_id={"seq": lax.rem(me + j, n)},
            device_id_type=MESH,
        )

    def qd_copy(j, which):
        return pltpu.make_async_remote_copy(
            src_ref=(q_ref, dout_ref)[which],
            dst_ref=qd_buf.at[j - 1, which],
            send_sem=qd_send.at[j - 1, which],
            recv_sem=qd_recv.at[j - 1, which],
            device_id={"seq": lax.rem(me + n - j, n)},
            device_id_type=MESH,
        )

    def st_copy(j):
        return pltpu.make_async_remote_copy(
            src_ref=stat_own,
            dst_ref=stat_buf.at[j - 1],
            send_sem=st_send.at[j - 1],
            recv_sem=st_recv.at[j - 1],
            device_id={"seq": lax.rem(me + n - j, n)},
            device_id_type=MESH,
        )

    w_rows = w_ref.shape[0]

    def w_copy(j):
        return pltpu.make_async_remote_copy(
            src_ref=w_ref,
            dst_ref=w_all.at[me],
            send_sem=w_send.at[j - 1],
            recv_sem=w_recv.at[j - 1],
            device_id={"seq": lax.rem(me + j, n)},
            device_id_type=MESH,
        )

    def ab_copy(j):
        return pltpu.make_async_remote_copy(
            src_ref=ab_buf.at[rank],
            dst_ref=ab_buf.at[rank],
            send_sem=ab_send.at[j - 1],
            recv_sem=ab_recv.at[j - 1],
            device_id={"seq": first + lax.rem(rank + j, size)},
            device_id_type=MESH,
        )

    def carry_copy():
        return pltpu.make_async_remote_copy(
            src_ref=carry_out,
            dst_ref=carry_in,
            send_sem=c_send,
            recv_sem=c_recv,
            device_id={"seq": lax.rem(me + n - size, n)},
            device_id_type=MESH,
        )

    last_reach = min(reach, n - 1)
    near = min(size, last_reach)

    def start_offsets(low, high):
        for j in range(low, high + 1):
            @pl.when(me + j < n)
            def _():
                kv_copy(j, 0).start()
                kv_copy(j, 1).start()

            @pl.when(me - j >= 0)
            def _():
                qd_copy(j, 0).start()
                qd_copy(j, 1).start()
                st_copy(j).start()

    start_offsets(1, near)

    row_ids = lax.broadcasted_iota(jnp.int32, (total, total), 0)
    col_ids = lax.broadcasted_iota(jnp.int32, (total, total), 1)
    shift = BLOCK.bit_length() - 1
    same = lax.shift_right_logical(row_ids, shift) == lax.shift_right_logical(col_ids, shift)
    eye = row_ids == col_ids
    causal = same & (row_ids >= col_ids)
    strict = same & (row_ids > col_ids)

    def to_column(row):
        return row_sum(jnp.where(eye, row, 0.0))

    def to_row(column):
        return column_sum(jnp.where(eye, column, 0.0))

    def flat_row(ref):
        return jnp.concatenate([ref[h : h + 1, :] for h in range(heads)], axis=1)

    decay_row = flat_row(decay_ref)
    decay_col = to_column(decay_row)
    beta = to_column(flat_row(beta_ref))
    summed = row_sum(jnp.where(causal, decay_row, 0.0))
    summed_row = column_sum(jnp.where(same & (row_ids <= col_ids), decay_col, 0.0))
    whole = row_sum(jnp.where(same, decay_row, 0.0))
    growth = jnp.exp(summed)
    tail = jnp.exp(row_sum(jnp.where(same & (row_ids < col_ids), decay_row, 0.0)))
    end_growth = jnp.exp(whole)
    raw_q = stack_heads(gq_ref[...], heads).astype(F32)
    raw_k = stack_heads(gk_ref[...], heads).astype(F32)
    values = stack_heads(gv_ref[...], heads).astype(F32)
    out_grad = stack_heads(gdo_ref[...], heads).astype(F32)
    inv_q = lax.rsqrt(row_sum(raw_q * raw_q) + EPS)
    inv_k = lax.rsqrt(row_sum(raw_k * raw_k) + EPS)
    scaling = depth ** (-0.5)
    unit_q = raw_q * inv_q * scaling
    unit_k = raw_k * inv_k
    fading = jnp.where(causal, jnp.exp(jnp.where(causal, summed - summed_row, 0.0)), 0.0)
    products = mm(jnp.concatenate([unit_k, unit_q], axis=0), unit_k, NT)
    key_products = products[:total]
    query_products = products[total:]
    strict_fading = jnp.where(strict, fading, 0.0)
    faded_keys = strict_fading * key_products
    lower = beta * faded_keys
    solved = jnp.where(eye, 1.0, 0.0) - lower
    powered = mm_full(lower, lower)
    for step in range(BLOCK.bit_length() - 2):
        if step < BLOCK.bit_length() - 3:
            both = mm_full(jnp.concatenate([solved, powered], axis=0), powered)
            solved = solved + both[:total]
            powered = both[total:]
        else:
            solved = solved + mm_full(solved, powered)
    attention = fading * query_products
    widened = mm(solved, (beta * growth) * unit_k)
    pulled = mm(attention, out_grad, TN)
    tailing = tail * unit_k
    grown_q = growth * unit_q

    def part(matrix, h, b):
        start = h * rows + b * BLOCK
        return matrix[start : start + BLOCK]

    depth_eye = jnp.where(
        lax.broadcasted_iota(jnp.int32, (depth, depth), 0)
        == lax.broadcasted_iota(jnp.int32, (depth, depth), 1),
        1.0,
        0.0,
    )
    for h in range(heads):
        across = None
        for b in reversed(range(blocks)):
            wide = part(widened, h, b)
            right = jnp.concatenate([part(tailing, h, b), part(pulled, h, b)], axis=1)
            product = mm(wide, right, TN)
            carry_map = part(end_growth, h, b)[0:1, :] * depth_eye - product[:, :depth]
            local = mm(part(grown_q, h, b), part(out_grad, h, b), TN) - product[:, depth:]
            map_buf[h, b, :, :depth] = carry_map
            map_buf[h, b, :, depth:] = local
            if across is None:
                across, offset = carry_map, local
            else:
                joined = mm(carry_map, jnp.concatenate([across, offset], axis=1))
                across, offset = joined[:, :depth], joined[:, depth:] + local
        ab_buf[rank, h, :, :depth] = (across - depth_eye).astype(BF16)
        ab_buf[rank, h, :, depth:] = offset.astype(BF16)

    key_ids = lax.broadcasted_iota(jnp.int32, (rows, rows), 0)
    query_ids = lax.broadcasted_iota(jnp.int32, (rows, rows), 1)

    def pair_terms(keys, vals, queries, grads, lse, dots, mask):
        logits = dot(keys, queries, NT) * scaling
        shifted = logits - lse
        if mask is None:
            chances = jnp.exp(shifted)
        else:
            chances = jnp.where(mask, jnp.exp(jnp.where(mask, shifted, 0.0)), 0.0)
        grad_prob = dot(vals, grads, NT)
        return (chances * (grad_prob - dots)).astype(BF16), chances.astype(BF16)

    def cut(ref_value, h):
        return ref_value[:, h * depth : (h + 1) * depth]

    for h in range(heads):
        grad_logit, weights = pair_terms(
            cut(k_ref, h), cut(v_ref, h), cut(q_ref, h), cut(dout_ref, h),
            stat_own[h : h + 1, :], stat_own[heads + h : heads + h + 1, :], query_ids >= key_ids,
        )
        cols = slice(h * depth, (h + 1) * depth)
        dq_acc[:, cols] = dot(grad_logit, cut(k_ref, h), TN)
        dkv_acc[:, cols] = dot(grad_logit, cut(q_ref, h))
        dkv_acc[:, columns + h * depth : columns + (h + 1) * depth] = dot(weights, cut(dout_ref, h))

    for j in range(1, size):
        ab_copy(j).start()
    start_offsets(near + 1, last_reach)
    for j in range(1, n):
        w_copy(j).start()

    def attend(low, high):
        for j in range(low, high + 1):
            mask = query_ids + j * rows - key_ids < WINDOW if (j + 1) * rows > WINDOW else None

            @pl.when(me - j >= 0)
            def _():
                kv_copy(j, 0).wait_recv()
                kv_copy(j, 1).wait_recv()
                for h in range(heads):
                    cols = slice(h * depth, (h + 1) * depth)
                    keys = kv_buf[j - 1, 0, :, cols]
                    grad_logit, _ = pair_terms(
                        keys, kv_buf[j - 1, 1, :, cols], cut(q_ref, h), cut(dout_ref, h),
                        stat_own[h : h + 1, :], stat_own[heads + h : heads + h + 1, :], mask,
                    )
                    dq_acc[:, cols] += dot(grad_logit, keys, TN)

            @pl.when(me + j < n)
            def _():
                qd_copy(j, 0).wait_recv()
                qd_copy(j, 1).wait_recv()
                st_copy(j).wait_recv()
                for h in range(heads):
                    cols = slice(h * depth, (h + 1) * depth)
                    queries = qd_buf[j - 1, 0, :, cols]
                    grads = qd_buf[j - 1, 1, :, cols]
                    grad_logit, weights = pair_terms(
                        cut(k_ref, h), cut(v_ref, h), queries, grads,
                        stat_buf[j - 1, h : h + 1, :],
                        stat_buf[j - 1, heads + h : heads + h + 1, :], mask,
                    )
                    dkv_acc[:, cols] += dot(grad_logit, queries)
                    dkv_acc[:, columns + h * depth : columns + (h + 1) * depth] += dot(
                        weights, grads
                    )

    for j in range(1, size):
        ab_copy(j).wait_recv()
    inside = []
    for h in range(heads):
        joined = jnp.concatenate([depth_eye, jnp.zeros((depth, depth), F32)], axis=1)
        suffix = joined
        for r in reversed(range(size)):
            suffix = jnp.where(rank == r, joined, suffix)
            change = ab_buf[r, h, :, :depth]
            later = joined
            high, low = split(later)
            joined = later + (dot(change, high) + dot(change, low))
            joined = jnp.concatenate(
                [joined[:, :depth], joined[:, depth:] + ab_buf[r, h, :, depth:].astype(F32)], axis=1
            )
        inside.append((joined, suffix))

    @pl.when(group == groups - 1)
    def _():
        carry_in[...] = jnp.zeros_like(carry_in)

    if groups > 1:
        @pl.when(group < groups - 1)
        def _():
            carry_copy().wait_recv()

    for h in range(heads):
        joined, _ = inside[h]
        high, low = split(joined[:, :depth])
        state = carry_in[h]
        carry_out[h] = (dot(high, state) + dot(low, state) + joined[:, depth:]).astype(BF16)
    if groups > 1:
        @pl.when(group > 0)
        def _():
            carry_copy().start()

    later = {}
    for h in range(heads):
        _, suffix = inside[h]
        high, low = split(suffix[:, :depth])
        state = carry_in[h]
        adjoint = dot(high, state) + dot(low, state) + suffix[:, depth:]
        for b in reversed(range(blocks)):
            later[h, b] = adjoint
            if b > 0:
                adjoint = mm(map_buf[h, b, :, :depth], adjoint) + map_buf[h, b, :, depth:]
    pairs = [(h, b) for h in range(heads) for b in range(blocks)]

    def by_parts(make):
        return jnp.concatenate([make(h, b) for h, b in pairs], axis=0)

    reads = [
        mm(jnp.concatenate([part(unit_k, h, b), part(unit_q, h, b)], axis=0), states_ref[b, h])
        for h, b in pairs
    ]
    key_reads = jnp.concatenate([item[:BLOCK] for item in reads], axis=0)
    query_reads = jnp.concatenate([item[BLOCK:] for item in reads], axis=0)
    remainder = values - growth * key_reads
    fresh = mm(solved, beta * remainder)
    fresh_grad = pulled + by_parts(lambda h, b: mm(part(tailing, h, b), later[h, b]))
    solved_grad = mm(solved, fresh_grad, TN)
    outer = mm(jnp.concatenate([out_grad, solved_grad], axis=0), fresh, NT)
    faded_grad = fading * outer[:total]
    lower_grad = -outer[total:]
    key_products_grad = beta * strict_fading * lower_grad
    value_grad = beta * solved_grad
    backs = [
        mm(
            jnp.concatenate([part(out_grad, h, b), part(value_grad, h, b)], axis=0),
            states_ref[b, h],
            NT,
        )
        for h, b in pairs
    ]
    out_back = jnp.concatenate([item[:BLOCK] for item in backs], axis=0)
    value_back = jnp.concatenate([item[BLOCK:] for item in backs], axis=0)
    fresh_back = tail * by_parts(lambda h, b: mm(part(fresh, h, b), later[h, b], NT))
    unit_q_grad = growth * out_back + mm(faded_grad, unit_k)
    unit_k_grad = (
        fresh_back
        - growth * value_back
        + mm(faded_grad, unit_q, TN)
        + mm(key_products_grad, unit_k)
        + mm(key_products_grad, unit_k, TN)
    )
    q_grad = scaling * inv_q * (unit_q_grad - raw_q * (inv_q * inv_q * row_sum(unit_q_grad * raw_q)))
    k_grad = inv_k * (unit_k_grad - raw_k * (inv_k * inv_k * row_sum(unit_k_grad * raw_k)))
    for h in range(heads):
        cols = slice(h * depth, (h + 1) * depth)
        own = slice(h * rows, (h + 1) * rows)
        gdq_out[:, cols] = q_grad[own].astype(BF16)
        gdk_out[:, cols] = k_grad[own].astype(BF16)
        gdv_out[:, cols] = value_grad[own].astype(BF16)
    beta_grad = row_sum(solved_grad * remainder) + row_sum(lower_grad * faded_keys)
    exponent = faded_grad * query_products + key_products_grad * key_products
    tail_grad = row_sum(unit_k * fresh_back)
    growth_grad = row_sum(out_grad * query_reads) - row_sum(value_grad * key_reads)
    summed_grad = (
        row_sum(exponent) - to_column(column_sum(exponent)) - tail_grad + growth * growth_grad
    )
    end_grad = end_growth * by_parts(
        lambda h, b: jnp.broadcast_to(
            column_sum(row_sum(later[h, b] * states_ref[b, h])), (BLOCK, 1)
        )
    )
    decay_grad = (
        column_sum(jnp.where(causal, summed_grad, 0.0))
        + column_sum(jnp.where(same, tail_grad, 0.0))
        + to_row(end_grad)
    )
    beta_row = to_row(beta_grad)
    for h in range(heads):
        own = slice(h * rows, (h + 1) * rows)
        gdecay_out[h : h + 1, :] = decay_grad[:, own]
        gbeta_out[h : h + 1, :] = beta_row[:, own]

    attend(1, last_reach)

    dq_out[...] = (dq_acc[...] * scaling).astype(BF16)
    both_grads = jnp.concatenate(
        [(dkv_acc[:, :columns] * scaling).astype(BF16), dkv_acc[:, columns:].astype(BF16)], axis=1
    )
    w_all[me] = w_ref[...]
    for j in range(1, n):
        w_copy(j).wait_recv()
    out_rows = dx_out.shape[0]
    pieces_each = out_rows // w_rows

    def dx_rows(owner):
        piece = w_all[pl.ds(owner * pieces_each, pieces_each)].reshape(out_rows, 2 * columns)
        return dot(piece, both_grads, NT)

    def dx_copy(j):
        return pltpu.make_async_remote_copy(
            src_ref=dx_send.at[j - 1],
            dst_ref=dx_recv.at[j - 1],
            send_sem=x_send.at[j - 1],
            recv_sem=x_recv.at[j - 1],
            device_id={"head": lax.rem(my_head + j, head_n)},
            device_id_type=MESH,
        )

    for j in range(1, head_n):
        dx_send[j - 1] = dx_rows(lax.rem(my_head + j, head_n))
        dx_copy(j).start()
    result = dx_rows(my_head)
    for j in range(1, head_n):
        dx_copy(j).wait_recv()
        result = result + dx_recv[j - 1]
    dx_out[...] = result.astype(BF16)

    for j in range(1, last_reach + 1):
        @pl.when(me + j < n)
        def _():
            kv_copy(j, 0).wait_send()
            kv_copy(j, 1).wait_send()

        @pl.when(me - j >= 0)
        def _():
            qd_copy(j, 0).wait_send()
            qd_copy(j, 1).wait_send()
            st_copy(j).wait_send()

    for j in range(1, n):
        w_copy(j).wait_send()
    for j in range(1, size):
        ab_copy(j).wait_send()
    if groups > 1:
        @pl.when(group > 0)
        def _():
            carry_copy().wait_send()

    for j in range(1, head_n):
        dx_copy(j).wait_send()


def per_device(n, head_n, *args):
    attn_q, attn_lse, w_kv, states = args[0], args[5], args[6], args[13]
    rows, columns = attn_q.shape
    heads = attn_lse.shape[0]
    depth = columns // heads
    reach = min(WINDOW // rows, n - 1)
    size = group_size(n)
    blocks = states.shape[0]
    w_rows = w_kv.shape[0]
    out_rows = n * w_rows // head_n
    args = list(args)
    args[6] = w_kv.reshape(w_rows, 2 * columns)
    dma = pltpu.SemaphoreType.DMA
    vmem = pl.BlockSpec(memory_space=pltpu.VMEM)
    others = max(head_n - 1, 1)
    return pl.pallas_call(
        functools.partial(kernel, n, head_n),
        out_shape=(
            jax.ShapeDtypeStruct((rows, columns), BF16),
            jax.ShapeDtypeStruct((out_rows, rows), BF16),
            jax.ShapeDtypeStruct((rows, columns), BF16),
            jax.ShapeDtypeStruct((rows, columns), BF16),
            jax.ShapeDtypeStruct((rows, columns), BF16),
            jax.ShapeDtypeStruct((heads, rows), F32),
            jax.ShapeDtypeStruct((heads, rows), F32),
        ),
        in_specs=[vmem] * len(args),
        out_specs=(vmem,) * 7,
        scratch_shapes=[
            pltpu.VMEM((reach, 2, rows, columns), BF16),
            pltpu.VMEM((reach, 2, rows, columns), BF16),
            pltpu.VMEM((2 * heads, rows), F32),
            pltpu.VMEM((reach, 2 * heads, rows), F32),
            pltpu.VMEM((n, w_rows, 2 * columns), BF16),
            pltpu.VMEM((size, heads, depth, 2 * depth), BF16),
            pltpu.VMEM((heads, depth, depth), BF16),
            pltpu.VMEM((heads, depth, depth), BF16),
            pltpu.VMEM((others, out_rows, rows), F32),
            pltpu.VMEM((others, out_rows, rows), F32),
            pltpu.VMEM((rows, columns), F32),
            pltpu.VMEM((rows, 2 * columns), F32),
            pltpu.VMEM((heads, blocks, depth, 2 * depth), F32),
            dma((reach, 2)), dma((reach, 2)),
            dma((reach, 2)), dma((reach, 2)),
            dma((reach,)), dma((reach,)),
            dma((n,)), dma((n,)),
            dma((size,)), dma((size,)),
            dma, dma,
            dma((others,)), dma((others,)),
        ],
        compiler_params=pltpu.CompilerParams(
            collective_id=0, has_side_effects=True, vmem_limit_bytes=60000000
        ),
        name="layer_backward",
    )(*args)


def solution(mesh):
    rows = P("seq", "head")
    gates = P("head", "seq")
    return jax.shard_map(
        functools.partial(per_device, mesh.shape["seq"], mesh.shape["head"]),
        mesh=mesh,
        in_specs=(
            rows, rows, rows, rows, rows, gates, P("seq", None, "head"),
            rows, rows, rows, rows, gates, gates, P("seq", "head", None, None),
        ),
        out_specs=(rows, gates, rows, rows, rows, gates, gates),
        check_vma=False,
    )
```

```python
import functools
import jax
import jax.numpy as jnp
from jax import lax
from jax.experimental import pallas as pl
from jax.experimental.pallas import tpu as pltpu
from jax.sharding import PartitionSpec as P

BLOCK = 64
WINDOW = 1024
EPS = 1e-06
MESH = pl.DeviceIdType.MESH
F32 = jnp.float32
BF16 = jnp.bfloat16

NN = (((1,), (0,)), ((), ()))
NT = (((1,), (1,)), ((), ()))
TN = (((0,), (0,)), ((), ()))


def dot(left, right, dims=NN):
    return lax.dot_general(left, right, dims, preferred_element_type=F32)


def split(matrix):
    high = matrix.astype(BF16)
    return high, (matrix - high.astype(F32)).astype(BF16)


def mm(left, right, dims=NN):
    left_high, left_low = split(left)
    right_high, right_low = split(right)
    return dot(left_high, right_high, dims) + (
        dot(left_high, right_low, dims) + dot(left_low, right_high, dims)
    )


def mm_full(left, right, dims=NN):
    return lax.dot_general(
        left, right, dims, precision=lax.Precision.HIGHEST, preferred_element_type=F32
    )


def row_sum(matrix):
    return jnp.sum(matrix, axis=1, keepdims=True)


def column_sum(matrix):
    return jnp.sum(matrix, axis=0, keepdims=True)


def stack_heads(matrix, heads):
    depth = matrix.shape[1] // heads
    return jnp.concatenate([matrix[:, h * depth : (h + 1) * depth] for h in range(heads)], axis=0)


def group_size(count, reach):
    size = 1
    while size * size < count:
        size *= 2
    while count % size or reach % size:
        size //= 2
    return size


def kernel(
    n,
    head_n,
    q_ref, k_ref, v_ref, out_ref, dout_ref, lse_ref, w_ref,
    gq_ref, gk_ref, gv_ref, gdo_ref, decay_ref, beta_ref, states_ref,
    dq_out, dx_out, gdq_out, gdk_out, gdv_out, gdecay_out, gbeta_out,
    kv_buf, qd_buf, stat_own, stat_buf, w_all, ab_buf, carry_in, carry_out, dx_send, dx_recv,
    dq_acc, dkv_acc, map_buf,
    kv_send, kv_recv, qd_send, qd_recv, st_send, st_recv, w_send, w_recv,
    kv_pass, qd_pass, st_pass, w_pass,
    ab_send, ab_recv, c_send, c_recv, x_send, x_recv,
):
    me = lax.axis_index("seq")
    my_head = lax.axis_index("head")
    rows, columns = q_ref.shape
    heads = lse_ref.shape[0]
    depth = columns // heads
    reach = WINDOW // rows
    blocks = rows // BLOCK
    total = heads * rows
    size = group_size(n, WINDOW // rows)
    groups = n // size
    rank = lax.rem(me, size)
    group = lax.div(me, size)
    first = group * size

    barrier = pltpu.get_barrier_semaphore()
    for j in range(1, n):
        pl.semaphore_signal(
            barrier, inc=1, device_id={"seq": lax.rem(me + j, n)}, device_id_type=MESH
        )
    for j in range(1, head_n):
        pl.semaphore_signal(
            barrier, inc=1, device_id={"head": lax.rem(my_head + j, head_n)}, device_id_type=MESH
        )

    ones = jnp.ones((8, depth), F32)
    for h in range(heads):
        cols = slice(h * depth, (h + 1) * depth)
        product = dout_ref[:, cols].astype(F32) * out_ref[:, cols].astype(F32)
        stat_own[h : h + 1, :] = lse_ref[h : h + 1, :]
        stat_own[heads + h : heads + h + 1, :] = mm_full(ones, product, NT)[0:1, :]
    pl.semaphore_wait(barrier, n - 1 + head_n - 1)

    hops = min(reach // size, groups - 1)

    def move(source, target, sent, received, index):
        return pltpu.make_async_remote_copy(
            src_ref=source,
            dst_ref=target,
            send_sem=sent,
            recv_sem=received,
            device_id={"seq": index},
            device_id_type=MESH,
        )

    def kv_copies(j):
        index = lax.rem(me + j, n)
        return [
            move(
                (k_ref, v_ref)[i], kv_buf.at[j - 1, i],
                kv_send.at[j - 1, i], kv_recv.at[j - 1, i], index,
            )
            for i in range(2)
        ]

    def qd_copies(j):
        index = lax.rem(me + n - j, n)
        return [
            move(
                (q_ref, dout_ref)[i], qd_buf.at[j - 1, i],
                qd_send.at[j - 1, i], qd_recv.at[j - 1, i], index,
            )
            for i in range(2)
        ] + [move(stat_own, stat_buf.at[j - 1], st_send.at[j - 1], st_recv.at[j - 1], index)]

    def kv_passes(m, i):
        peer = lax.rem(rank + i, size)
        slot = m * size + peer - rank - 1
        return [
            move(
                kv_buf.at[m * size - 1, c], kv_buf.at[slot, c],
                kv_pass.at[m - 1, i, c], kv_recv.at[slot, c], first + peer,
            )
            for c in range(2)
        ]

    def qd_passes(m, i):
        peer = lax.rem(rank + i, size)
        slot = m * size + rank - peer - 1
        return [
            move(
                qd_buf.at[m * size - 1, c], qd_buf.at[slot, c],
                qd_pass.at[m - 1, i, c], qd_recv.at[slot, c], first + peer,
            )
            for c in range(2)
        ] + [
            move(
                stat_buf.at[m * size - 1], stat_buf.at[slot],
                st_pass.at[m - 1, i], st_recv.at[slot], first + peer,
            )
        ]

    def kv_goes(m, i):
        peer = lax.rem(rank + i, size)
        return (group >= m) & (m * size + peer - rank <= reach)

    def qd_goes(m, i):
        peer = lax.rem(rank + i, size)
        return (group + m < groups) & (m * size + rank - peer <= reach)

    w_rows = w_ref.shape[0]

    def w_copy(m):
        return move(
            w_ref, w_all.at[me], w_send.at[m - 1], w_recv.at[0, m], lax.rem(me + m * size, n)
        )

    def w_passes(i):
        peer = lax.rem(rank + i, size)
        return [
            move(
                w_ref if m == 0 else w_all.at[lax.rem(me + n - m * size, n)],
                w_all.at[lax.rem(me + n - m * size, n)],
                w_pass.at[i, m], w_recv.at[i, m], first + peer,
            )
            for m in range(groups)
        ]

    def each(copies, act):
        for copy in copies:
            getattr(copy, act)()

    def own_copies(act):
        for m in range(1, hops + 1):
            @pl.when(group + m < groups)
            def _():
                each(kv_copies(m * size), act)

            @pl.when(group >= m)
            def _():
                each(qd_copies(m * size), act)

        for j in range(1, size):
            @pl.when(rank + j < size)
            def _():
                each(kv_copies(j), act)

            @pl.when(rank >= j)
            def _():
                each(qd_copies(j), act)

    def pass_copies(m, act):
        for i in range(1, size):
            @pl.when(kv_goes(m, i))
            def _():
                each(kv_passes(m, i), act)

            @pl.when(qd_goes(m, i))
            def _():
                each(qd_passes(m, i), act)

    def take_column(m):
        @pl.when(group >= m)
        def _():
            each(kv_copies(m * size), "wait_recv")

        @pl.when(group + m < groups)
        def _():
            each(qd_copies(m * size), "wait_recv")

    def ab_copy(j):
        return pltpu.make_async_remote_copy(
            src_ref=ab_buf.at[rank],
            dst_ref=ab_buf.at[rank],
            send_sem=ab_send.at[j - 1],
            recv_sem=ab_recv.at[j - 1],
            device_id={"seq": first + lax.rem(rank + j, size)},
            device_id_type=MESH,
        )

    def carry_copy():
        return pltpu.make_async_remote_copy(
            src_ref=carry_out,
            dst_ref=carry_in,
            send_sem=c_send,
            recv_sem=c_recv,
            device_id={"seq": lax.rem(me + n - size, n)},
            device_id_type=MESH,
        )

    own_copies("start")
    for m in range(1, groups):
        w_copy(m).start()

    row_ids = lax.broadcasted_iota(jnp.int32, (total, total), 0)
    col_ids = lax.broadcasted_iota(jnp.int32, (total, total), 1)
    shift = BLOCK.bit_length() - 1
    same = lax.shift_right_logical(row_ids, shift) == lax.shift_right_logical(col_ids, shift)
    eye = row_ids == col_ids
    causal = same & (row_ids >= col_ids)
    strict = same & (row_ids > col_ids)

    def to_column(row):
        return row_sum(jnp.where(eye, row, 0.0))

    def to_row(column):
        return column_sum(jnp.where(eye, column, 0.0))

    def flat_row(ref):
        return jnp.concatenate([ref[h : h + 1, :] for h in range(heads)], axis=1)

    decay_row = flat_row(decay_ref)
    decay_col = to_column(decay_row)
    beta = to_column(flat_row(beta_ref))
    summed = row_sum(jnp.where(causal, decay_row, 0.0))
    summed_row = column_sum(jnp.where(same & (row_ids <= col_ids), decay_col, 0.0))
    whole = row_sum(jnp.where(same, decay_row, 0.0))
    growth = jnp.exp(summed)
    tail = jnp.exp(row_sum(jnp.where(same & (row_ids < col_ids), decay_row, 0.0)))
    end_growth = jnp.exp(whole)
    raw_q = stack_heads(gq_ref[...], heads).astype(F32)
    raw_k = stack_heads(gk_ref[...], heads).astype(F32)
    values = stack_heads(gv_ref[...], heads).astype(F32)
    out_grad = stack_heads(gdo_ref[...], heads).astype(F32)
    inv_q = lax.rsqrt(row_sum(raw_q * raw_q) + EPS)
    inv_k = lax.rsqrt(row_sum(raw_k * raw_k) + EPS)
    scaling = depth ** (-0.5)
    unit_q = raw_q * inv_q * scaling
    unit_k = raw_k * inv_k
    fading = jnp.where(causal, jnp.exp(jnp.where(causal, summed - summed_row, 0.0)), 0.0)
    products = mm(jnp.concatenate([unit_k, unit_q], axis=0), unit_k, NT)
    key_products = products[:total]
    query_products = products[total:]
    strict_fading = jnp.where(strict, fading, 0.0)
    faded_keys = strict_fading * key_products
    lower = beta * faded_keys
    solved = jnp.where(eye, 1.0, 0.0) - lower
    powered = mm_full(lower, lower)
    for step in range(BLOCK.bit_length() - 2):
        if step < BLOCK.bit_length() - 3:
            both = mm_full(jnp.concatenate([solved, powered], axis=0), powered)
            solved = solved + both[:total]
            powered = both[total:]
        else:
            solved = solved + mm_full(solved, powered)
    attention = fading * query_products
    widened = mm(solved, (beta * growth) * unit_k)
    pulled = mm(attention, out_grad, TN)
    tailing = tail * unit_k
    grown_q = growth * unit_q

    def part(matrix, h, b):
        start = h * rows + b * BLOCK
        return matrix[start : start + BLOCK]

    depth_eye = jnp.where(
        lax.broadcasted_iota(jnp.int32, (depth, depth), 0)
        == lax.broadcasted_iota(jnp.int32, (depth, depth), 1),
        1.0,
        0.0,
    )
    for h in range(heads):
        across = None
        for b in reversed(range(blocks)):
            wide = part(widened, h, b)
            right = jnp.concatenate([part(tailing, h, b), part(pulled, h, b)], axis=1)
            product = mm(wide, right, TN)
            carry_map = part(end_growth, h, b)[0:1, :] * depth_eye - product[:, :depth]
            local = mm(part(grown_q, h, b), part(out_grad, h, b), TN) - product[:, depth:]
            map_buf[h, b, :, :depth] = carry_map
            map_buf[h, b, :, depth:] = local
            if across is None:
                across, offset = carry_map, local
            else:
                joined = mm(carry_map, jnp.concatenate([across, offset], axis=1))
                across, offset = joined[:, :depth], joined[:, depth:] + local
        ab_buf[rank, h, :, :depth] = (across - depth_eye).astype(BF16)
        ab_buf[rank, h, :, depth:] = offset.astype(BF16)

    key_ids = lax.broadcasted_iota(jnp.int32, (rows, rows), 0)
    query_ids = lax.broadcasted_iota(jnp.int32, (rows, rows), 1)

    def pair_terms(keys, vals, queries, grads, lse, dots, mask):
        logits = dot(keys, queries, NT) * scaling
        shifted = logits - lse
        if mask is None:
            chances = jnp.exp(shifted)
        else:
            chances = jnp.where(mask, jnp.exp(jnp.where(mask, shifted, 0.0)), 0.0)
        grad_prob = dot(vals, grads, NT)
        return (chances * (grad_prob - dots)).astype(BF16), chances.astype(BF16)

    def cut(ref_value, h):
        return ref_value[:, h * depth : (h + 1) * depth]

    for h in range(heads):
        grad_logit, weights = pair_terms(
            cut(k_ref, h), cut(v_ref, h), cut(q_ref, h), cut(dout_ref, h),
            stat_own[h : h + 1, :], stat_own[heads + h : heads + h + 1, :], query_ids >= key_ids,
        )
        cols = slice(h * depth, (h + 1) * depth)
        dq_acc[:, cols] = dot(grad_logit, cut(k_ref, h), TN)
        dkv_acc[:, cols] = dot(grad_logit, cut(q_ref, h))
        dkv_acc[:, columns + h * depth : columns + (h + 1) * depth] = dot(weights, cut(dout_ref, h))

    for j in range(1, size):
        ab_copy(j).start()
    for m in range(1, hops + 1):
        take_column(m)
        pass_copies(m, "start")
    for m in range(1, groups):
        w_copy(m).wait_recv()
    for i in range(1, size):
        each(w_passes(i), "start")

    def attend(distances, keys_here, queries_here):
        for j in distances:
            mask = query_ids + j * rows - key_ids < WINDOW if (j + 1) * rows > WINDOW else None

            @pl.when(keys_here(j))
            def _():
                if j % size:
                    each(kv_copies(j), "wait_recv")
                for h in range(heads):
                    cols = slice(h * depth, (h + 1) * depth)
                    keys = kv_buf[j - 1, 0, :, cols]
                    grad_logit, _ = pair_terms(
                        keys, kv_buf[j - 1, 1, :, cols], cut(q_ref, h), cut(dout_ref, h),
                        stat_own[h : h + 1, :], stat_own[heads + h : heads + h + 1, :], mask,
                    )
                    dq_acc[:, cols] += dot(grad_logit, keys, TN)

            @pl.when(queries_here(j))
            def _():
                if j % size:
                    each(qd_copies(j), "wait_recv")
                for h in range(heads):
                    cols = slice(h * depth, (h + 1) * depth)
                    queries = qd_buf[j - 1, 0, :, cols]
                    grads = qd_buf[j - 1, 1, :, cols]
                    grad_logit, weights = pair_terms(
                        cut(k_ref, h), cut(v_ref, h), queries, grads,
                        stat_buf[j - 1, h : h + 1, :],
                        stat_buf[j - 1, heads + h : heads + h + 1, :], mask,
                    )
                    dkv_acc[:, cols] += dot(grad_logit, queries)
                    dkv_acc[:, columns + h * depth : columns + (h + 1) * depth] += dot(
                        weights, grads
                    )

    attend(range(1, size), lambda j: rank >= j, lambda j: rank + j < size)
    attend(
        range(size, hops * size + 1, size), lambda j: me >= j, lambda j: me + j < n
    )

    pairs = [(h, b) for h in range(heads) for b in range(blocks)]

    def by_parts(make):
        return jnp.concatenate([make(h, b) for h, b in pairs], axis=0)

    reads = [
        mm(jnp.concatenate([part(unit_k, h, b), part(unit_q, h, b)], axis=0), states_ref[b, h])
        for h, b in pairs
    ]
    key_reads = jnp.concatenate([item[:BLOCK] for item in reads], axis=0)
    query_reads = jnp.concatenate([item[BLOCK:] for item in reads], axis=0)
    remainder = values - growth * key_reads
    fresh = mm(solved, beta * remainder)
    faded_grad = fading * mm(out_grad, fresh, NT)
    out_back = by_parts(lambda h, b: mm(part(out_grad, h, b), states_ref[b, h], NT))
    unit_q_grad = growth * out_back + mm(faded_grad, unit_k)
    faded_back = mm(faded_grad, unit_q, TN)

    for j in range(1, size):
        ab_copy(j).wait_recv()
    inside = []
    for h in range(heads):
        joined = jnp.concatenate([depth_eye, jnp.zeros((depth, depth), F32)], axis=1)
        suffix = joined
        for r in reversed(range(size)):
            suffix = jnp.where(rank == r, joined, suffix)
            change = ab_buf[r, h, :, :depth]
            later = joined
            high, low = split(later)
            joined = later + (dot(change, high) + dot(change, low))
            joined = jnp.concatenate(
                [joined[:, :depth], joined[:, depth:] + ab_buf[r, h, :, depth:].astype(F32)], axis=1
            )
        inside.append((joined, suffix))

    @pl.when(group == groups - 1)
    def _():
        carry_in[...] = jnp.zeros_like(carry_in)

    if groups > 1:
        @pl.when(group < groups - 1)
        def _():
            carry_copy().wait_recv()

    for h in range(heads):
        joined, _ = inside[h]
        high, low = split(joined[:, :depth])
        state = carry_in[h]
        carry_out[h] = (dot(high, state) + dot(low, state) + joined[:, depth:]).astype(BF16)
    if groups > 1:
        @pl.when(group > 0)
        def _():
            carry_copy().start()

    later = {}
    for h in range(heads):
        _, suffix = inside[h]
        high, low = split(suffix[:, :depth])
        state = carry_in[h]
        adjoint = dot(high, state) + dot(low, state) + suffix[:, depth:]
        for b in reversed(range(blocks)):
            later[h, b] = adjoint
            if b > 0:
                adjoint = mm(map_buf[h, b, :, :depth], adjoint) + map_buf[h, b, :, depth:]
    fresh_grad = pulled + by_parts(lambda h, b: mm(part(tailing, h, b), later[h, b]))
    solved_grad = mm(solved, fresh_grad, TN)
    lower_grad = -mm(solved_grad, fresh, NT)
    key_products_grad = beta * strict_fading * lower_grad
    value_grad = beta * solved_grad
    value_back = by_parts(lambda h, b: mm(part(value_grad, h, b), states_ref[b, h], NT))
    fresh_back = tail * by_parts(lambda h, b: mm(part(fresh, h, b), later[h, b], NT))
    unit_k_grad = (
        fresh_back
        - growth * value_back
        + faded_back
        + mm(key_products_grad, unit_k)
        + mm(key_products_grad, unit_k, TN)
    )
    q_grad = scaling * inv_q * (unit_q_grad - raw_q * (inv_q * inv_q * row_sum(unit_q_grad * raw_q)))
    k_grad = inv_k * (unit_k_grad - raw_k * (inv_k * inv_k * row_sum(unit_k_grad * raw_k)))
    for h in range(heads):
        cols = slice(h * depth, (h + 1) * depth)
        own = slice(h * rows, (h + 1) * rows)
        gdq_out[:, cols] = q_grad[own].astype(BF16)
        gdk_out[:, cols] = k_grad[own].astype(BF16)
        gdv_out[:, cols] = value_grad[own].astype(BF16)
    beta_grad = row_sum(solved_grad * remainder) + row_sum(lower_grad * faded_keys)
    exponent = faded_grad * query_products + key_products_grad * key_products
    tail_grad = row_sum(unit_k * fresh_back)
    growth_grad = row_sum(out_grad * query_reads) - row_sum(value_grad * key_reads)
    summed_grad = (
        row_sum(exponent) - to_column(column_sum(exponent)) - tail_grad + growth * growth_grad
    )
    end_grad = end_growth * by_parts(
        lambda h, b: jnp.broadcast_to(
            column_sum(row_sum(later[h, b] * states_ref[b, h])), (BLOCK, 1)
        )
    )
    decay_grad = (
        column_sum(jnp.where(causal, summed_grad, 0.0))
        + column_sum(jnp.where(same, tail_grad, 0.0))
        + to_row(end_grad)
    )
    beta_row = to_row(beta_grad)
    for h in range(heads):
        own = slice(h * rows, (h + 1) * rows)
        gdecay_out[h : h + 1, :] = decay_grad[:, own]
        gbeta_out[h : h + 1, :] = beta_row[:, own]

    attend(
        [j for j in range(1, min(reach, n - 1) + 1) if j % size],
        lambda j: (me >= j) & (rank < j),
        lambda j: (me + j < n) & (rank + j >= size),
    )

    dq_out[...] = (dq_acc[...] * scaling).astype(BF16)
    both_grads = jnp.concatenate(
        [(dkv_acc[:, :columns] * scaling).astype(BF16), dkv_acc[:, columns:].astype(BF16)], axis=1
    )
    w_all[me] = w_ref[...]
    for i in range(1, size):
        each(w_passes(i), "wait_recv")
    out_rows = dx_out.shape[0]
    pieces_each = out_rows // w_rows

    def dx_rows(owner):
        piece = w_all[pl.ds(owner * pieces_each, pieces_each)].reshape(out_rows, 2 * columns)
        return dot(piece, both_grads, NT)

    def dx_copy(j):
        return pltpu.make_async_remote_copy(
            src_ref=dx_send.at[j - 1],
            dst_ref=dx_recv.at[j - 1],
            send_sem=x_send.at[j - 1],
            recv_sem=x_recv.at[j - 1],
            device_id={"head": lax.rem(my_head + j, head_n)},
            device_id_type=MESH,
        )

    for j in range(1, head_n):
        dx_send[j - 1] = dx_rows(lax.rem(my_head + j, head_n))
        dx_copy(j).start()
    result = dx_rows(my_head)
    for j in range(1, head_n):
        dx_copy(j).wait_recv()
        result = result + dx_recv[j - 1]
    dx_out[...] = result.astype(BF16)

    own_copies("wait_send")
    for m in range(1, hops + 1):
        pass_copies(m, "wait_send")
    for m in range(1, groups):
        w_copy(m).wait_send()
    for i in range(1, size):
        each(w_passes(i), "wait_send")
    for j in range(1, size):
        ab_copy(j).wait_send()
    if groups > 1:
        @pl.when(group > 0)
        def _():
            carry_copy().wait_send()

    for j in range(1, head_n):
        dx_copy(j).wait_send()


def hand_over(*refs):
    half = len(refs) // 2
    for source, target in zip(refs[:half], refs[half:]):
        target[...] = source[...]


def per_device(n, head_n, *args):
    attn_q, attn_lse, w_kv, states = args[0], args[5], args[6], args[13]
    rows, columns = attn_q.shape
    heads = attn_lse.shape[0]
    depth = columns // heads
    reach = min(WINDOW // rows, n - 1)
    size = group_size(n, WINDOW // rows)
    blocks = states.shape[0]
    groups = n // size
    hops = max(min(reach // size, groups - 1), 1)
    w_rows = w_kv.shape[0]
    out_rows = n * w_rows // head_n
    args = list(args)
    args[6] = w_kv.reshape(w_rows, 2 * columns)
    dma = pltpu.SemaphoreType.DMA
    vmem = pl.BlockSpec(memory_space=pltpu.VMEM)
    others = max(head_n - 1, 1)
    results = pl.pallas_call(
        functools.partial(kernel, n, head_n),
        out_shape=(
            jax.ShapeDtypeStruct((rows, columns), BF16),
            jax.ShapeDtypeStruct((out_rows, rows), BF16),
            jax.ShapeDtypeStruct((rows, columns), BF16),
            jax.ShapeDtypeStruct((rows, columns), BF16),
            jax.ShapeDtypeStruct((rows, columns), BF16),
            jax.ShapeDtypeStruct((heads, rows), F32),
            jax.ShapeDtypeStruct((heads, rows), F32),
        ),
        in_specs=[vmem] * len(args),
        out_specs=(vmem,) * 7,
        scratch_shapes=[
            pltpu.VMEM((reach, 2, rows, columns), BF16),
            pltpu.VMEM((reach, 2, rows, columns), BF16),
            pltpu.VMEM((2 * heads, rows), F32),
            pltpu.VMEM((reach, 2 * heads, rows), F32),
            pltpu.VMEM((n, w_rows, 2 * columns), BF16),
            pltpu.VMEM((size, heads, depth, 2 * depth), BF16),
            pltpu.VMEM((heads, depth, depth), BF16),
            pltpu.VMEM((heads, depth, depth), BF16),
            pltpu.VMEM((others, out_rows, rows), F32),
            pltpu.VMEM((others, out_rows, rows), F32),
            pltpu.VMEM((rows, columns), F32),
            pltpu.VMEM((rows, 2 * columns), F32),
            pltpu.VMEM((heads, blocks, depth, 2 * depth), F32),
            dma((reach, 2)), dma((reach, 2)),
            dma((reach, 2)), dma((reach, 2)),
            dma((reach,)), dma((reach,)),
            dma((groups,)), dma((size, groups)),
            dma((hops, size, 2)), dma((hops, size, 2)), dma((hops, size)), dma((size, groups)),
            dma((size,)), dma((size,)),
            dma, dma,
            dma((others,)), dma((others,)),
        ],
        compiler_params=pltpu.CompilerParams(
            collective_id=0, has_side_effects=True, vmem_limit_bytes=60000000
        ),
        name="layer_backward",
    )(*args)
    return pl.pallas_call(
        hand_over,
        out_shape=[jax.ShapeDtypeStruct(item.shape, item.dtype) for item in results],
        in_specs=[vmem] * len(results),
        out_specs=[vmem] * len(results),
        name="hand_over",
    )(*results)


def solution(mesh):
    rows = P("seq", "head")
    gates = P("head", "seq")
    return jax.shard_map(
        functools.partial(per_device, mesh.shape["seq"], mesh.shape["head"]),
        mesh=mesh,
        in_specs=(
            rows, rows, rows, rows, rows, gates, P("seq", None, "head"),
            rows, rows, rows, rows, gates, gates, P("seq", "head", None, None),
        ),
        out_specs=(rows, gates, rows, rows, rows, gates, gates),
        check_vma=False,
    )
```

```python
import functools
import jax
import jax.numpy as jnp
from jax import lax
from jax.experimental import pallas as pl
from jax.experimental.pallas import tpu as pltpu
from jax.sharding import PartitionSpec as P

BLOCK = 64
WINDOW = 1024
EPS = 1e-06
MESH = pl.DeviceIdType.MESH
F32 = jnp.float32
BF16 = jnp.bfloat16

NN = (((1,), (0,)), ((), ()))
NT = (((1,), (1,)), ((), ()))
TN = (((0,), (0,)), ((), ()))


def dot(left, right, dims=NN):
    return lax.dot_general(left, right, dims, preferred_element_type=F32)


def split(matrix):
    high = matrix.astype(BF16)
    return high, (matrix - high.astype(F32)).astype(BF16)


def mm(left, right, dims=NN):
    left_high, left_low = split(left)
    right_high, right_low = split(right)
    return dot(left_high, right_high, dims) + (
        dot(left_high, right_low, dims) + dot(left_low, right_high, dims)
    )


def mm_once(left, right, dims=NN):
    return dot(left.astype(BF16), right.astype(BF16), dims)


def mm_full(left, right, dims=NN):
    return lax.dot_general(
        left, right, dims, precision=lax.Precision.HIGHEST, preferred_element_type=F32
    )


def row_sum(matrix):
    return jnp.sum(matrix, axis=1, keepdims=True)


def column_sum(matrix):
    return jnp.sum(matrix, axis=0, keepdims=True)


def stack_heads(matrix, heads):
    depth = matrix.shape[1] // heads
    return jnp.concatenate([matrix[:, h * depth : (h + 1) * depth] for h in range(heads)], axis=0)


def group_size(count, reach):
    size = 1
    while size * size < count:
        size *= 2
    while count % size or reach % size:
        size //= 2
    return size


def kernel(
    n,
    head_n,
    q_ref, k_ref, v_ref, out_ref, dout_ref, lse_ref, w_ref,
    gq_ref, gk_ref, gv_ref, gdo_ref, decay_ref, beta_ref, states_ref,
    dq_out, dx_out, gdq_out, gdk_out, gdv_out, gdecay_out, gbeta_out,
    kv_buf, qd_buf, stat_own, stat_buf, w_all, ab_buf, carry_in, carry_out, dx_send, dx_recv,
    dq_acc, dkv_acc, map_buf,
    kv_send, kv_recv, qd_send, qd_recv, st_send, st_recv, w_send, w_recv,
    kv_pass, qd_pass, st_pass, w_pass,
    ab_send, ab_recv, c_send, c_recv, x_send, x_recv,
):
    me = lax.axis_index("seq")
    my_head = lax.axis_index("head")
    rows, columns = q_ref.shape
    heads = lse_ref.shape[0]
    depth = columns // heads
    reach = WINDOW // rows
    blocks = rows // BLOCK
    total = heads * rows
    size = group_size(n, WINDOW // rows)
    groups = n // size
    rank = lax.rem(me, size)
    group = lax.div(me, size)
    first = group * size

    barrier = pltpu.get_barrier_semaphore()
    for j in range(1, n):
        pl.semaphore_signal(
            barrier, inc=1, device_id={"seq": lax.rem(me + j, n)}, device_id_type=MESH
        )
    for j in range(1, head_n):
        pl.semaphore_signal(
            barrier, inc=1, device_id={"head": lax.rem(my_head + j, head_n)}, device_id_type=MESH
        )

    ones = jnp.ones((8, depth), F32)
    for h in range(heads):
        cols = slice(h * depth, (h + 1) * depth)
        product = dout_ref[:, cols].astype(F32) * out_ref[:, cols].astype(F32)
        stat_own[h : h + 1, :] = lse_ref[h : h + 1, :]
        stat_own[heads + h : heads + h + 1, :] = mm_full(ones, product, NT)[0:1, :]
    pl.semaphore_wait(barrier, n - 1 + head_n - 1)

    hops = min(reach // size, groups - 1)

    def move(source, target, sent, received, index):
        return pltpu.make_async_remote_copy(
            src_ref=source,
            dst_ref=target,
            send_sem=sent,
            recv_sem=received,
            device_id={"seq": index},
            device_id_type=MESH,
        )

    def kv_copies(j):
        index = lax.rem(me + j, n)
        return [
            move(
                (k_ref, v_ref)[i], kv_buf.at[j - 1, i],
                kv_send.at[j - 1, i], kv_recv.at[j - 1, i], index,
            )
            for i in range(2)
        ]

    def qd_copies(j):
        index = lax.rem(me + n - j, n)
        return [
            move(
                (q_ref, dout_ref)[i], qd_buf.at[j - 1, i],
                qd_send.at[j - 1, i], qd_recv.at[j - 1, i], index,
            )
            for i in range(2)
        ] + [move(stat_own, stat_buf.at[j - 1], st_send.at[j - 1], st_recv.at[j - 1], index)]

    def kv_passes(m, i):
        peer = lax.rem(rank + i, size)
        slot = m * size + peer - rank - 1
        return [
            move(
                kv_buf.at[m * size - 1, c], kv_buf.at[slot, c],
                kv_pass.at[m - 1, i, c], kv_recv.at[slot, c], first + peer,
            )
            for c in range(2)
        ]

    def qd_passes(m, i):
        peer = lax.rem(rank + i, size)
        slot = m * size + rank - peer - 1
        return [
            move(
                qd_buf.at[m * size - 1, c], qd_buf.at[slot, c],
                qd_pass.at[m - 1, i, c], qd_recv.at[slot, c], first + peer,
            )
            for c in range(2)
        ] + [
            move(
                stat_buf.at[m * size - 1], stat_buf.at[slot],
                st_pass.at[m - 1, i], st_recv.at[slot], first + peer,
            )
        ]

    def kv_goes(m, i):
        peer = lax.rem(rank + i, size)
        return (group >= m) & (m * size + peer - rank <= reach)

    def qd_goes(m, i):
        peer = lax.rem(rank + i, size)
        return (group + m < groups) & (m * size + rank - peer <= reach)

    w_rows = w_ref.shape[0]

    def w_copy(m):
        return move(
            w_ref, w_all.at[me], w_send.at[m - 1], w_recv.at[0, m], lax.rem(me + m * size, n)
        )

    def w_passes(i):
        peer = lax.rem(rank + i, size)
        return [
            move(
                w_ref if m == 0 else w_all.at[lax.rem(me + n - m * size, n)],
                w_all.at[lax.rem(me + n - m * size, n)],
                w_pass.at[i, m], w_recv.at[i, m], first + peer,
            )
            for m in range(groups)
        ]

    def each(copies, act):
        for copy in copies:
            getattr(copy, act)()

    def own_copies(act):
        for m in range(1, hops + 1):
            @pl.when(group + m < groups)
            def _():
                each(kv_copies(m * size), act)

            @pl.when(group >= m)
            def _():
                each(qd_copies(m * size), act)

        for j in range(1, size):
            @pl.when(rank + j < size)
            def _():
                each(kv_copies(j), act)

            @pl.when(rank >= j)
            def _():
                each(qd_copies(j), act)

    def pass_keys(m, act):
        for i in range(1, size):
            @pl.when(kv_goes(m, i))
            def _():
                each(kv_passes(m, i), act)

    def pass_queries(m, act):
        for i in range(1, size):
            @pl.when(qd_goes(m, i))
            def _():
                each(qd_passes(m, i), act)

    def take_keys(m):
        @pl.when(group >= m)
        def _():
            each(kv_copies(m * size), "wait_recv")

    def take_queries(m):
        @pl.when(group + m < groups)
        def _():
            each(qd_copies(m * size), "wait_recv")

    def ab_copy(j):
        return pltpu.make_async_remote_copy(
            src_ref=ab_buf.at[rank],
            dst_ref=ab_buf.at[rank],
            send_sem=ab_send.at[j - 1],
            recv_sem=ab_recv.at[j - 1],
            device_id={"seq": first + lax.rem(rank + j, size)},
            device_id_type=MESH,
        )

    def carry_copy():
        return pltpu.make_async_remote_copy(
            src_ref=carry_out,
            dst_ref=carry_in,
            send_sem=c_send,
            recv_sem=c_recv,
            device_id={"seq": lax.rem(me + n - size, n)},
            device_id_type=MESH,
        )

    own_copies("start")
    for m in range(1, groups):
        w_copy(m).start()

    row_ids = lax.broadcasted_iota(jnp.int32, (total, total), 0)
    col_ids = lax.broadcasted_iota(jnp.int32, (total, total), 1)
    shift = BLOCK.bit_length() - 1
    same = lax.shift_right_logical(row_ids, shift) == lax.shift_right_logical(col_ids, shift)
    eye = row_ids == col_ids
    causal = same & (row_ids >= col_ids)
    strict = same & (row_ids > col_ids)

    def to_column(row):
        return row_sum(jnp.where(eye, row, 0.0))

    def to_row(column):
        return column_sum(jnp.where(eye, column, 0.0))

    def flat_row(ref):
        return jnp.concatenate([ref[h : h + 1, :] for h in range(heads)], axis=1)

    decay_row = flat_row(decay_ref)
    decay_col = to_column(decay_row)
    beta = to_column(flat_row(beta_ref))
    summed = row_sum(jnp.where(causal, decay_row, 0.0))
    summed_row = column_sum(jnp.where(same & (row_ids <= col_ids), decay_col, 0.0))
    whole = row_sum(jnp.where(same, decay_row, 0.0))
    growth = jnp.exp(summed)
    tail = jnp.exp(row_sum(jnp.where(same & (row_ids < col_ids), decay_row, 0.0)))
    end_growth = jnp.exp(whole)
    raw_q = stack_heads(gq_ref[...], heads).astype(F32)
    raw_k = stack_heads(gk_ref[...], heads).astype(F32)
    values = stack_heads(gv_ref[...], heads).astype(F32)
    out_grad = stack_heads(gdo_ref[...], heads).astype(F32)
    inv_q = lax.rsqrt(row_sum(raw_q * raw_q) + EPS)
    inv_k = lax.rsqrt(row_sum(raw_k * raw_k) + EPS)
    scaling = depth ** (-0.5)
    unit_q = raw_q * inv_q * scaling
    unit_k = raw_k * inv_k
    fading = jnp.where(causal, jnp.exp(jnp.where(causal, summed - summed_row, 0.0)), 0.0)
    products = mm(jnp.concatenate([unit_k, unit_q], axis=0), unit_k, NT)
    key_products = products[:total]
    query_products = products[total:]
    strict_fading = jnp.where(strict, fading, 0.0)
    faded_keys = strict_fading * key_products
    lower = beta * faded_keys
    solved = jnp.where(eye, 1.0, 0.0) - lower
    powered = mm(lower, lower)
    for step in range(BLOCK.bit_length() - 2):
        if step < BLOCK.bit_length() - 3:
            both = mm(jnp.concatenate([solved, powered], axis=0), powered)
            solved = solved + both[:total]
            powered = both[total:]
        else:
            solved = solved + mm(solved, powered)
    if hops:
        take_keys(1)
        pass_keys(1, "start")
    attention = fading * query_products
    widened = mm(solved, (beta * growth) * unit_k)
    pulled = mm(attention, out_grad, TN)
    tailing = tail * unit_k
    grown_q = growth * unit_q

    def part(matrix, h, b):
        start = h * rows + b * BLOCK
        return matrix[start : start + BLOCK]

    depth_eye = jnp.where(
        lax.broadcasted_iota(jnp.int32, (depth, depth), 0)
        == lax.broadcasted_iota(jnp.int32, (depth, depth), 1),
        1.0,
        0.0,
    )
    for h in range(heads):
        across = None
        for b in reversed(range(blocks)):
            wide = part(widened, h, b)
            right = jnp.concatenate([part(tailing, h, b), part(pulled, h, b)], axis=1)
            product = mm(wide, right, TN)
            carry_map = part(end_growth, h, b)[0:1, :] * depth_eye - product[:, :depth]
            local = mm(part(grown_q, h, b), part(out_grad, h, b), TN) - product[:, depth:]
            map_buf[h, b, :, :depth] = carry_map
            map_buf[h, b, :, depth:] = local
            if across is None:
                across, offset = carry_map, local
            else:
                joined = mm(carry_map, jnp.concatenate([across, offset], axis=1))
                across, offset = joined[:, :depth], joined[:, depth:] + local
        ab_buf[rank, h, :, :depth] = (across - depth_eye).astype(BF16)
        ab_buf[rank, h, :, depth:] = offset.astype(BF16)

    key_ids = lax.broadcasted_iota(jnp.int32, (rows, rows), 0)
    query_ids = lax.broadcasted_iota(jnp.int32, (rows, rows), 1)

    def pair_terms(keys, vals, queries, grads, lse, dots, mask):
        logits = dot(keys, queries, NT) * scaling
        shifted = logits - lse
        if mask is None:
            chances = jnp.exp(shifted)
        else:
            chances = jnp.where(mask, jnp.exp(jnp.where(mask, shifted, 0.0)), 0.0)
        grad_prob = dot(vals, grads, NT)
        return (chances * (grad_prob - dots)).astype(BF16), chances.astype(BF16)

    def cut(ref_value, h):
        return ref_value[:, h * depth : (h + 1) * depth]

    for h in range(heads):
        grad_logit, weights = pair_terms(
            cut(k_ref, h), cut(v_ref, h), cut(q_ref, h), cut(dout_ref, h),
            stat_own[h : h + 1, :], stat_own[heads + h : heads + h + 1, :], query_ids >= key_ids,
        )
        cols = slice(h * depth, (h + 1) * depth)
        dq_acc[:, cols] = dot(grad_logit, cut(k_ref, h), TN)
        dkv_acc[:, cols] = dot(grad_logit, cut(q_ref, h))
        dkv_acc[:, columns + h * depth : columns + (h + 1) * depth] = dot(weights, cut(dout_ref, h))

    for j in range(1, size):
        ab_copy(j).start()
    for m in range(1, hops + 1):
        if m > 1:
            take_keys(m)
            pass_keys(m, "start")
        take_queries(m)
        pass_queries(m, "start")
    for m in range(1, groups):
        w_copy(m).wait_recv()
    for i in range(1, size):
        each(w_passes(i), "start")

    def attend(distances, keys_here, queries_here):
        for j in distances:
            mask = query_ids + j * rows - key_ids < WINDOW if (j + 1) * rows > WINDOW else None

            @pl.when(keys_here(j))
            def _():
                if j % size:
                    each(kv_copies(j), "wait_recv")
                for h in range(heads):
                    cols = slice(h * depth, (h + 1) * depth)
                    keys = kv_buf[j - 1, 0, :, cols]
                    grad_logit, _ = pair_terms(
                        keys, kv_buf[j - 1, 1, :, cols], cut(q_ref, h), cut(dout_ref, h),
                        stat_own[h : h + 1, :], stat_own[heads + h : heads + h + 1, :], mask,
                    )
                    dq_acc[:, cols] += dot(grad_logit, keys, TN)

            @pl.when(queries_here(j))
            def _():
                if j % size:
                    each(qd_copies(j), "wait_recv")
                for h in range(heads):
                    cols = slice(h * depth, (h + 1) * depth)
                    queries = qd_buf[j - 1, 0, :, cols]
                    grads = qd_buf[j - 1, 1, :, cols]
                    grad_logit, weights = pair_terms(
                        cut(k_ref, h), cut(v_ref, h), queries, grads,
                        stat_buf[j - 1, h : h + 1, :],
                        stat_buf[j - 1, heads + h : heads + h + 1, :], mask,
                    )
                    dkv_acc[:, cols] += dot(grad_logit, queries)
                    dkv_acc[:, columns + h * depth : columns + (h + 1) * depth] += dot(
                        weights, grads
                    )

    attend(range(1, size), lambda j: rank >= j, lambda j: rank + j < size)
    attend(
        range(size, hops * size + 1, size), lambda j: me >= j, lambda j: me + j < n
    )

    pairs = [(h, b) for h in range(heads) for b in range(blocks)]

    def by_parts(make):
        return jnp.concatenate([make(h, b) for h, b in pairs], axis=0)

    reads = [
        mm(jnp.concatenate([part(unit_k, h, b), part(unit_q, h, b)], axis=0), states_ref[b, h])
        for h, b in pairs
    ]
    key_reads = jnp.concatenate([item[:BLOCK] for item in reads], axis=0)
    query_reads = jnp.concatenate([item[BLOCK:] for item in reads], axis=0)
    remainder = values - growth * key_reads
    fresh = mm(solved, beta * remainder)
    faded_grad = fading * mm(out_grad, fresh, NT)
    out_back = by_parts(lambda h, b: mm_once(part(out_grad, h, b), states_ref[b, h], NT))
    unit_q_grad = growth * out_back + mm_once(faded_grad, unit_k)
    faded_back = mm_once(faded_grad, unit_q, TN)

    for j in range(1, size):
        ab_copy(j).wait_recv()
    inside = []
    for h in range(heads):
        joined = jnp.concatenate([depth_eye, jnp.zeros((depth, depth), F32)], axis=1)
        suffix = joined
        for r in reversed(range(size)):
            suffix = jnp.where(rank == r, joined, suffix)
            change = ab_buf[r, h, :, :depth]
            later = joined
            high, low = split(later)
            joined = later + (dot(change, high) + dot(change, low))
            joined = jnp.concatenate(
                [joined[:, :depth], joined[:, depth:] + ab_buf[r, h, :, depth:].astype(F32)], axis=1
            )
        inside.append((joined, suffix))

    @pl.when(group == groups - 1)
    def _():
        carry_in[...] = jnp.zeros_like(carry_in)

    if groups > 1:
        @pl.when(group < groups - 1)
        def _():
            carry_copy().wait_recv()

    for h in range(heads):
        joined, _ = inside[h]
        high, low = split(joined[:, :depth])
        state = carry_in[h]
        carry_out[h] = (dot(high, state) + dot(low, state) + joined[:, depth:]).astype(BF16)
    if groups > 1:
        @pl.when(group > 0)
        def _():
            carry_copy().start()

    later = {}
    for h in range(heads):
        _, suffix = inside[h]
        high, low = split(suffix[:, :depth])
        state = carry_in[h]
        adjoint = dot(high, state) + dot(low, state) + suffix[:, depth:]
        for b in reversed(range(blocks)):
            later[h, b] = adjoint
            if b > 0:
                adjoint = mm(map_buf[h, b, :, :depth], adjoint) + map_buf[h, b, :, depth:]
    fresh_grad = pulled + by_parts(lambda h, b: mm(part(tailing, h, b), later[h, b]))
    solved_grad = mm(solved, fresh_grad, TN)
    lower_grad = -mm(solved_grad, fresh, NT)
    key_products_grad = beta * strict_fading * lower_grad
    value_grad = beta * solved_grad
    value_back = by_parts(lambda h, b: mm_once(part(value_grad, h, b), states_ref[b, h], NT))
    fresh_back = tail * by_parts(lambda h, b: mm(part(fresh, h, b), later[h, b], NT))
    unit_k_grad = (
        fresh_back
        - growth * value_back
        + faded_back
        + mm_once(key_products_grad, unit_k)
        + mm_once(key_products_grad, unit_k, TN)
    )
    q_grad = scaling * inv_q * (unit_q_grad - raw_q * (inv_q * inv_q * row_sum(unit_q_grad * raw_q)))
    k_grad = inv_k * (unit_k_grad - raw_k * (inv_k * inv_k * row_sum(unit_k_grad * raw_k)))
    for h in range(heads):
        cols = slice(h * depth, (h + 1) * depth)
        own = slice(h * rows, (h + 1) * rows)
        gdq_out[:, cols] = q_grad[own].astype(BF16)
        gdk_out[:, cols] = k_grad[own].astype(BF16)
        gdv_out[:, cols] = value_grad[own].astype(BF16)
    beta_grad = row_sum(solved_grad * remainder) + row_sum(lower_grad * faded_keys)
    exponent = faded_grad * query_products + key_products_grad * key_products
    tail_grad = row_sum(unit_k * fresh_back)
    growth_grad = row_sum(out_grad * query_reads) - row_sum(value_grad * key_reads)
    summed_grad = (
        row_sum(exponent) - to_column(column_sum(exponent)) - tail_grad + growth * growth_grad
    )
    end_grad = end_growth * by_parts(
        lambda h, b: jnp.broadcast_to(
            column_sum(row_sum(later[h, b] * states_ref[b, h])), (BLOCK, 1)
        )
    )
    decay_grad = (
        column_sum(jnp.where(causal, summed_grad, 0.0))
        + column_sum(jnp.where(same, tail_grad, 0.0))
        + to_row(end_grad)
    )
    beta_row = to_row(beta_grad)
    for h in range(heads):
        own = slice(h * rows, (h + 1) * rows)
        gdecay_out[h : h + 1, :] = decay_grad[:, own]
        gbeta_out[h : h + 1, :] = beta_row[:, own]

    attend(
        [j for j in range(1, min(reach, n - 1) + 1) if j % size],
        lambda j: (me >= j) & (rank < j),
        lambda j: (me + j < n) & (rank + j >= size),
    )

    dq_out[...] = (dq_acc[...] * scaling).astype(BF16)
    both_grads = jnp.concatenate(
        [(dkv_acc[:, :columns] * scaling).astype(BF16), dkv_acc[:, columns:].astype(BF16)], axis=1
    )
    w_all[me] = w_ref[...]
    for i in range(1, size):
        each(w_passes(i), "wait_recv")
    out_rows = dx_out.shape[0]
    pieces_each = out_rows // w_rows

    def dx_rows(owner):
        piece = w_all[pl.ds(owner * pieces_each, pieces_each)].reshape(out_rows, 2 * columns)
        return dot(piece, both_grads, NT)

    def dx_copy(j):
        return pltpu.make_async_remote_copy(
            src_ref=dx_send.at[j - 1],
            dst_ref=dx_recv.at[j - 1],
            send_sem=x_send.at[j - 1],
            recv_sem=x_recv.at[j - 1],
            device_id={"head": lax.rem(my_head + j, head_n)},
            device_id_type=MESH,
        )

    for j in range(1, head_n):
        dx_send[j - 1] = dx_rows(lax.rem(my_head + j, head_n))
        dx_copy(j).start()
    result = dx_rows(my_head)
    for j in range(1, head_n):
        dx_copy(j).wait_recv()
        result = result + dx_recv[j - 1]
    dx_out[...] = result.astype(BF16)

    own_copies("wait_send")
    for m in range(1, hops + 1):
        pass_keys(m, "wait_send")
        pass_queries(m, "wait_send")
    for m in range(1, groups):
        w_copy(m).wait_send()
    for i in range(1, size):
        each(w_passes(i), "wait_send")
    for j in range(1, size):
        ab_copy(j).wait_send()
    if groups > 1:
        @pl.when(group > 0)
        def _():
            carry_copy().wait_send()

    for j in range(1, head_n):
        dx_copy(j).wait_send()


def hand_over(*refs):
    half = len(refs) // 2
    for source, target in zip(refs[:half], refs[half:]):
        target[...] = source[...]


def per_device(n, head_n, *args):
    attn_q, attn_lse, w_kv, states = args[0], args[5], args[6], args[13]
    rows, columns = attn_q.shape
    heads = attn_lse.shape[0]
    depth = columns // heads
    reach = min(WINDOW // rows, n - 1)
    size = group_size(n, WINDOW // rows)
    blocks = states.shape[0]
    groups = n // size
    hops = max(min(reach // size, groups - 1), 1)
    w_rows = w_kv.shape[0]
    out_rows = n * w_rows // head_n
    args = list(args)
    args[6] = w_kv.reshape(w_rows, 2 * columns)
    dma = pltpu.SemaphoreType.DMA
    vmem = pl.BlockSpec(memory_space=pltpu.VMEM)
    others = max(head_n - 1, 1)
    results = pl.pallas_call(
        functools.partial(kernel, n, head_n),
        out_shape=(
            jax.ShapeDtypeStruct((rows, columns), BF16),
            jax.ShapeDtypeStruct((out_rows, rows), BF16),
            jax.ShapeDtypeStruct((rows, columns), BF16),
            jax.ShapeDtypeStruct((rows, columns), BF16),
            jax.ShapeDtypeStruct((rows, columns), BF16),
            jax.ShapeDtypeStruct((heads, rows), F32),
            jax.ShapeDtypeStruct((heads, rows), F32),
        ),
        in_specs=[vmem] * len(args),
        out_specs=(vmem,) * 7,
        scratch_shapes=[
            pltpu.VMEM((reach, 2, rows, columns), BF16),
            pltpu.VMEM((reach, 2, rows, columns), BF16),
            pltpu.VMEM((2 * heads, rows), F32),
            pltpu.VMEM((reach, 2 * heads, rows), F32),
            pltpu.VMEM((n, w_rows, 2 * columns), BF16),
            pltpu.VMEM((size, heads, depth, 2 * depth), BF16),
            pltpu.VMEM((heads, depth, depth), BF16),
            pltpu.VMEM((heads, depth, depth), BF16),
            pltpu.VMEM((others, out_rows, rows), F32),
            pltpu.VMEM((others, out_rows, rows), F32),
            pltpu.VMEM((rows, columns), F32),
            pltpu.VMEM((rows, 2 * columns), F32),
            pltpu.VMEM((heads, blocks, depth, 2 * depth), F32),
            dma((reach, 2)), dma((reach, 2)),
            dma((reach, 2)), dma((reach, 2)),
            dma((reach,)), dma((reach,)),
            dma((groups,)), dma((size, groups)),
            dma((hops, size, 2)), dma((hops, size, 2)), dma((hops, size)), dma((size, groups)),
            dma((size,)), dma((size,)),
            dma, dma,
            dma((others,)), dma((others,)),
        ],
        compiler_params=pltpu.CompilerParams(
            collective_id=0, has_side_effects=True, vmem_limit_bytes=60000000
        ),
        name="layer_backward",
    )(*args)
    return pl.pallas_call(
        hand_over,
        out_shape=[jax.ShapeDtypeStruct(item.shape, item.dtype) for item in results],
        in_specs=[vmem] * len(results),
        out_specs=[vmem] * len(results),
        name="hand_over",
    )(*results)


def solution(mesh):
    rows = P("seq", "head")
    gates = P("head", "seq")
    return jax.shard_map(
        functools.partial(per_device, mesh.shape["seq"], mesh.shape["head"]),
        mesh=mesh,
        in_specs=(
            rows, rows, rows, rows, rows, gates, P("seq", None, "head"),
            rows, rows, rows, rows, gates, gates, P("seq", "head", None, None),
        ),
        out_specs=(rows, gates, rows, rows, rows, gates, gates),
        check_vma=False,
    )
```

```python
import functools
import jax
import jax.numpy as jnp
from jax import lax
from jax.experimental import pallas as pl
from jax.experimental.pallas import tpu as pltpu
from jax.sharding import PartitionSpec as P

BLOCK = 64
WINDOW = 1024
EPS = 1e-06
MESH = pl.DeviceIdType.MESH
F32 = jnp.float32
BF16 = jnp.bfloat16

NN = (((1,), (0,)), ((), ()))
NT = (((1,), (1,)), ((), ()))
TN = (((0,), (0,)), ((), ()))


def dot(left, right, dims=NN):
    return lax.dot_general(left, right, dims, preferred_element_type=F32)


def split(matrix):
    high = matrix.astype(BF16)
    return high, (matrix - high.astype(F32)).astype(BF16)


def mm(left, right, dims=NN):
    left_high, left_low = split(left)
    right_high, right_low = split(right)
    return dot(left_high, right_high, dims) + (
        dot(left_high, right_low, dims) + dot(left_low, right_high, dims)
    )


def mm_once(left, right, dims=NN):
    return dot(left.astype(BF16), right.astype(BF16), dims)


def mm_full(left, right, dims=NN):
    return lax.dot_general(
        left, right, dims, precision=lax.Precision.HIGHEST, preferred_element_type=F32
    )


def row_sum(matrix):
    return jnp.sum(matrix, axis=1, keepdims=True)


def column_sum(matrix):
    return jnp.sum(matrix, axis=0, keepdims=True)


def stack_heads(matrix, heads):
    depth = matrix.shape[1] // heads
    return jnp.concatenate([matrix[:, h * depth : (h + 1) * depth] for h in range(heads)], axis=0)


def group_size(count, reach):
    size = 1
    while size * size < count:
        size *= 2
    while count % size or reach % size:
        size //= 2
    return size


def kernel(
    n,
    head_n,
    q_ref, k_ref, v_ref, out_ref, dout_ref, lse_ref, w_ref,
    gq_ref, gk_ref, gv_ref, gdo_ref, decay_ref, beta_ref, states_ref,
    dq_out, dx_out, gdq_out, gdk_out, gdv_out, gdecay_out, gbeta_out,
    kv_buf, qd_buf, stat_own, stat_buf, w_all, ab_buf, carry_in, carry_out, dx_send, dx_recv,
    dq_acc, dkv_acc, map_buf,
    kv_send, kv_recv, qd_send, qd_recv, st_send, st_recv, w_send, w_recv,
    kv_pass, qd_pass, st_pass, w_pass,
    ab_send, ab_recv, c_send, c_recv, x_send, x_recv,
):
    me = lax.axis_index("seq")
    my_head = lax.axis_index("head")
    rows, columns = q_ref.shape
    heads = lse_ref.shape[0]
    depth = columns // heads
    reach = WINDOW // rows
    blocks = rows // BLOCK
    total = heads * rows
    size = group_size(n, WINDOW // rows)
    groups = n // size
    rank = lax.rem(me, size)
    group = lax.div(me, size)
    first = group * size

    barrier = pltpu.get_barrier_semaphore()
    for j in range(1, n):
        pl.semaphore_signal(
            barrier, inc=1, device_id={"seq": lax.rem(me + j, n)}, device_id_type=MESH
        )
    for j in range(1, head_n):
        pl.semaphore_signal(
            barrier, inc=1, device_id={"head": lax.rem(my_head + j, head_n)}, device_id_type=MESH
        )

    ones = jnp.ones((8, depth), F32)
    for h in range(heads):
        cols = slice(h * depth, (h + 1) * depth)
        product = dout_ref[:, cols].astype(F32) * out_ref[:, cols].astype(F32)
        stat_own[h : h + 1, :] = lse_ref[h : h + 1, :]
        stat_own[heads + h : heads + h + 1, :] = mm_full(ones, product, NT)[0:1, :]
    pl.semaphore_wait(barrier, n - 1 + head_n - 1)

    hops = min(reach // size, groups - 1)

    def move(source, target, sent, received, index):
        return pltpu.make_async_remote_copy(
            src_ref=source,
            dst_ref=target,
            send_sem=sent,
            recv_sem=received,
            device_id={"seq": index},
            device_id_type=MESH,
        )

    def kv_copies(j):
        index = lax.rem(me + j, n)
        return [
            move(
                (k_ref, v_ref)[i], kv_buf.at[j - 1, i],
                kv_send.at[j - 1, i], kv_recv.at[j - 1, i], index,
            )
            for i in range(2)
        ]

    def qd_copies(j):
        index = lax.rem(me + n - j, n)
        return [
            move(
                (q_ref, dout_ref)[i], qd_buf.at[j - 1, i],
                qd_send.at[j - 1, i], qd_recv.at[j - 1, i], index,
            )
            for i in range(2)
        ] + [move(stat_own, stat_buf.at[j - 1], st_send.at[j - 1], st_recv.at[j - 1], index)]

    def kv_passes(m, i):
        peer = lax.rem(rank + i, size)
        slot = m * size + peer - rank - 1
        return [
            move(
                kv_buf.at[m * size - 1, c], kv_buf.at[slot, c],
                kv_pass.at[m - 1, i, c], kv_recv.at[slot, c], first + peer,
            )
            for c in range(2)
        ]

    def qd_passes(m, i):
        peer = lax.rem(rank + i, size)
        slot = m * size + rank - peer - 1
        return [
            move(
                qd_buf.at[m * size - 1, c], qd_buf.at[slot, c],
                qd_pass.at[m - 1, i, c], qd_recv.at[slot, c], first + peer,
            )
            for c in range(2)
        ] + [
            move(
                stat_buf.at[m * size - 1], stat_buf.at[slot],
                st_pass.at[m - 1, i], st_recv.at[slot], first + peer,
            )
        ]

    def kv_goes(m, i):
        peer = lax.rem(rank + i, size)
        return (group >= m) & (m * size + peer - rank <= reach)

    def qd_goes(m, i):
        peer = lax.rem(rank + i, size)
        return (group + m < groups) & (m * size + rank - peer <= reach)

    w_rows = w_ref.shape[0]

    def w_copy(m):
        return move(
            w_ref, w_all.at[me], w_send.at[m - 1], w_recv.at[0, m], lax.rem(me + m * size, n)
        )

    def w_passes(i):
        peer = lax.rem(rank + i, size)
        return [
            move(
                w_ref if m == 0 else w_all.at[lax.rem(me + n - m * size, n)],
                w_all.at[lax.rem(me + n - m * size, n)],
                w_pass.at[i, m], w_recv.at[i, m], first + peer,
            )
            for m in range(groups)
        ]

    def each(copies, act):
        for copy in copies:
            getattr(copy, act)()

    def own_copies(act):
        for m in range(1, hops + 1):
            @pl.when(group + m < groups)
            def _():
                each(kv_copies(m * size), act)

            @pl.when(group >= m)
            def _():
                each(qd_copies(m * size), act)

        for j in range(1, size):
            @pl.when(rank + j < size)
            def _():
                each(kv_copies(j), act)

            @pl.when(rank >= j)
            def _():
                each(qd_copies(j), act)

    def pass_keys(m, act):
        for i in range(1, size):
            @pl.when(kv_goes(m, i))
            def _():
                each(kv_passes(m, i), act)

    def pass_queries(m, act):
        for i in range(1, size):
            @pl.when(qd_goes(m, i))
            def _():
                each(qd_passes(m, i), act)

    def take_keys(m):
        @pl.when(group >= m)
        def _():
            each(kv_copies(m * size), "wait_recv")

    def take_queries(m):
        @pl.when(group + m < groups)
        def _():
            each(qd_copies(m * size), "wait_recv")

    def ab_copy(j):
        return pltpu.make_async_remote_copy(
            src_ref=ab_buf.at[rank],
            dst_ref=ab_buf.at[rank],
            send_sem=ab_send.at[j - 1],
            recv_sem=ab_recv.at[j - 1],
            device_id={"seq": first + lax.rem(rank + j, size)},
            device_id_type=MESH,
        )

    def carry_copy():
        return pltpu.make_async_remote_copy(
            src_ref=carry_out,
            dst_ref=carry_in,
            send_sem=c_send,
            recv_sem=c_recv,
            device_id={"seq": lax.rem(me + n - size, n)},
            device_id_type=MESH,
        )

    own_copies("start")
    for m in range(1, groups):
        w_copy(m).start()

    row_ids = lax.broadcasted_iota(jnp.int32, (total, total), 0)
    col_ids = lax.broadcasted_iota(jnp.int32, (total, total), 1)
    shift = BLOCK.bit_length() - 1
    same = lax.shift_right_logical(row_ids, shift) == lax.shift_right_logical(col_ids, shift)
    eye = row_ids == col_ids
    causal = same & (row_ids >= col_ids)
    strict = same & (row_ids > col_ids)

    def to_column(row):
        return row_sum(jnp.where(eye, row, 0.0))

    def to_row(column):
        return column_sum(jnp.where(eye, column, 0.0))

    def flat_row(ref):
        return jnp.concatenate([ref[h : h + 1, :] for h in range(heads)], axis=1)

    decay_row = flat_row(decay_ref)
    decay_col = to_column(decay_row)
    beta = to_column(flat_row(beta_ref))
    summed = row_sum(jnp.where(causal, decay_row, 0.0))
    summed_row = column_sum(jnp.where(same & (row_ids <= col_ids), decay_col, 0.0))
    whole = row_sum(jnp.where(same, decay_row, 0.0))
    growth = jnp.exp(summed)
    tail = jnp.exp(row_sum(jnp.where(same & (row_ids < col_ids), decay_row, 0.0)))
    end_growth = jnp.exp(whole)
    raw_q = stack_heads(gq_ref[...], heads).astype(F32)
    raw_k = stack_heads(gk_ref[...], heads).astype(F32)
    values = stack_heads(gv_ref[...], heads).astype(F32)
    out_grad = stack_heads(gdo_ref[...], heads).astype(F32)
    inv_q = lax.rsqrt(row_sum(raw_q * raw_q) + EPS)
    inv_k = lax.rsqrt(row_sum(raw_k * raw_k) + EPS)
    scaling = depth ** (-0.5)
    unit_q = raw_q * inv_q * scaling
    unit_k = raw_k * inv_k
    fading = jnp.where(causal, jnp.exp(jnp.where(causal, summed - summed_row, 0.0)), 0.0)
    products = mm(jnp.concatenate([unit_k, unit_q], axis=0), unit_k, NT)
    key_products = products[:total]
    query_products = products[total:]
    strict_fading = jnp.where(strict, fading, 0.0)
    faded_keys = strict_fading * key_products
    lower = beta * faded_keys
    solved = jnp.where(eye, 1.0, 0.0) - lower
    powered = mm(lower, lower)
    for step in range(BLOCK.bit_length() - 2):
        if step < BLOCK.bit_length() - 3:
            both = mm(jnp.concatenate([solved, powered], axis=0), powered)
            solved = solved + both[:total]
            powered = both[total:]
        else:
            solved = solved + mm(solved, powered)
    early = group < groups - 2

    if hops:
        @pl.when(early)
        def _():
            take_keys(1)
            pass_keys(1, "start")

    attention = fading * query_products
    widened = mm(solved, (beta * growth) * unit_k)
    pulled = mm(attention, out_grad, TN)
    tailing = tail * unit_k
    grown_q = growth * unit_q

    def part(matrix, h, b):
        start = h * rows + b * BLOCK
        return matrix[start : start + BLOCK]

    depth_eye = jnp.where(
        lax.broadcasted_iota(jnp.int32, (depth, depth), 0)
        == lax.broadcasted_iota(jnp.int32, (depth, depth), 1),
        1.0,
        0.0,
    )
    for h in range(heads):
        across = None
        for b in reversed(range(blocks)):
            wide = part(widened, h, b)
            right = jnp.concatenate([part(tailing, h, b), part(pulled, h, b)], axis=1)
            product = mm(wide, right, TN)
            carry_map = part(end_growth, h, b)[0:1, :] * depth_eye - product[:, :depth]
            local = mm(part(grown_q, h, b), part(out_grad, h, b), TN) - product[:, depth:]
            map_buf[h, b, :, :depth] = carry_map
            map_buf[h, b, :, depth:] = local
            if across is None:
                across, offset = carry_map, local
            else:
                joined = mm(carry_map, jnp.concatenate([across, offset], axis=1))
                across, offset = joined[:, :depth], joined[:, depth:] + local
        ab_buf[rank, h, :, :depth] = (across - depth_eye).astype(BF16)
        ab_buf[rank, h, :, depth:] = offset.astype(BF16)

    key_ids = lax.broadcasted_iota(jnp.int32, (rows, rows), 0)
    query_ids = lax.broadcasted_iota(jnp.int32, (rows, rows), 1)

    def pair_terms(keys, vals, queries, grads, lse, dots, mask):
        logits = dot(keys, queries, NT) * scaling
        shifted = logits - lse
        if mask is None:
            chances = jnp.exp(shifted)
        else:
            chances = jnp.where(mask, jnp.exp(jnp.where(mask, shifted, 0.0)), 0.0)
        grad_prob = dot(vals, grads, NT)
        return (chances * (grad_prob - dots)).astype(BF16), chances.astype(BF16)

    def cut(ref_value, h):
        return ref_value[:, h * depth : (h + 1) * depth]

    for h in range(heads):
        grad_logit, weights = pair_terms(
            cut(k_ref, h), cut(v_ref, h), cut(q_ref, h), cut(dout_ref, h),
            stat_own[h : h + 1, :], stat_own[heads + h : heads + h + 1, :], query_ids >= key_ids,
        )
        cols = slice(h * depth, (h + 1) * depth)
        dq_acc[:, cols] = dot(grad_logit, cut(k_ref, h), TN)
        dkv_acc[:, cols] = dot(grad_logit, cut(q_ref, h))
        dkv_acc[:, columns + h * depth : columns + (h + 1) * depth] = dot(weights, cut(dout_ref, h))

    for j in range(1, size):
        ab_copy(j).start()
    for m in range(1, hops + 1):
        if m > 1:
            take_keys(m)
            pass_keys(m, "start")
        else:
            @pl.when(jnp.logical_not(early))
            def _():
                take_keys(1)
                pass_keys(1, "start")

        take_queries(m)
        pass_queries(m, "start")
    for m in range(1, groups):
        w_copy(m).wait_recv()
    for i in range(1, size):
        each(w_passes(i), "start")

    def attend(distances, keys_here, queries_here):
        for j in distances:
            mask = query_ids + j * rows - key_ids < WINDOW if (j + 1) * rows > WINDOW else None

            @pl.when(keys_here(j))
            def _():
                if j % size:
                    each(kv_copies(j), "wait_recv")
                for h in range(heads):
                    cols = slice(h * depth, (h + 1) * depth)
                    keys = kv_buf[j - 1, 0, :, cols]
                    grad_logit, _ = pair_terms(
                        keys, kv_buf[j - 1, 1, :, cols], cut(q_ref, h), cut(dout_ref, h),
                        stat_own[h : h + 1, :], stat_own[heads + h : heads + h + 1, :], mask,
                    )
                    dq_acc[:, cols] += dot(grad_logit, keys, TN)

            @pl.when(queries_here(j))
            def _():
                if j % size:
                    each(qd_copies(j), "wait_recv")
                for h in range(heads):
                    cols = slice(h * depth, (h + 1) * depth)
                    queries = qd_buf[j - 1, 0, :, cols]
                    grads = qd_buf[j - 1, 1, :, cols]
                    grad_logit, weights = pair_terms(
                        cut(k_ref, h), cut(v_ref, h), queries, grads,
                        stat_buf[j - 1, h : h + 1, :],
                        stat_buf[j - 1, heads + h : heads + h + 1, :], mask,
                    )
                    dkv_acc[:, cols] += dot(grad_logit, queries)
                    dkv_acc[:, columns + h * depth : columns + (h + 1) * depth] += dot(
                        weights, grads
                    )

    attend(range(1, size), lambda j: rank >= j, lambda j: rank + j < size)
    attend(
        range(size, hops * size + 1, size), lambda j: me >= j, lambda j: me + j < n
    )

    pairs = [(h, b) for h in range(heads) for b in range(blocks)]

    def by_parts(make):
        return jnp.concatenate([make(h, b) for h, b in pairs], axis=0)

    reads = [
        mm(jnp.concatenate([part(unit_k, h, b), part(unit_q, h, b)], axis=0), states_ref[b, h])
        for h, b in pairs
    ]
    key_reads = jnp.concatenate([item[:BLOCK] for item in reads], axis=0)
    query_reads = jnp.concatenate([item[BLOCK:] for item in reads], axis=0)
    remainder = values - growth * key_reads
    fresh = mm(solved, beta * remainder)
    faded_grad = fading * mm(out_grad, fresh, NT)
    out_back = by_parts(lambda h, b: mm_once(part(out_grad, h, b), states_ref[b, h], NT))
    unit_q_grad = growth * out_back + mm_once(faded_grad, unit_k)
    faded_back = mm_once(faded_grad, unit_q, TN)

    for j in range(1, size):
        ab_copy(j).wait_recv()
    inside = []
    for h in range(heads):
        joined = jnp.concatenate([depth_eye, jnp.zeros((depth, depth), F32)], axis=1)
        suffix = joined
        for r in reversed(range(size)):
            suffix = jnp.where(rank == r, joined, suffix)
            change = ab_buf[r, h, :, :depth]
            later = joined
            high, low = split(later)
            joined = later + (dot(change, high) + dot(change, low))
            joined = jnp.concatenate(
                [joined[:, :depth], joined[:, depth:] + ab_buf[r, h, :, depth:].astype(F32)], axis=1
            )
        inside.append((joined, suffix))

    @pl.when(group == groups - 1)
    def _():
        carry_in[...] = jnp.zeros_like(carry_in)

    if groups > 1:
        @pl.when(group < groups - 1)
        def _():
            carry_copy().wait_recv()

    for h in range(heads):
        joined, _ = inside[h]
        high, low = split(joined[:, :depth])
        state = carry_in[h]
        carry_out[h] = (dot(high, state) + dot(low, state) + joined[:, depth:]).astype(BF16)
    if groups > 1:
        @pl.when(group > 0)
        def _():
            carry_copy().start()

    later = {}
    for h in range(heads):
        _, suffix = inside[h]
        high, low = split(suffix[:, :depth])
        state = carry_in[h]
        adjoint = dot(high, state) + dot(low, state) + suffix[:, depth:]
        for b in reversed(range(blocks)):
            later[h, b] = adjoint
            if b > 0:
                adjoint = mm(map_buf[h, b, :, :depth], adjoint) + map_buf[h, b, :, depth:]
    fresh_grad = pulled + by_parts(lambda h, b: mm(part(tailing, h, b), later[h, b]))
    solved_grad = mm(solved, fresh_grad, TN)
    lower_grad = -mm(solved_grad, fresh, NT)
    key_products_grad = beta * strict_fading * lower_grad
    value_grad = beta * solved_grad
    value_back = by_parts(lambda h, b: mm_once(part(value_grad, h, b), states_ref[b, h], NT))
    fresh_back = tail * by_parts(lambda h, b: mm(part(fresh, h, b), later[h, b], NT))
    unit_k_grad = (
        fresh_back
        - growth * value_back
        + faded_back
        + mm_once(key_products_grad, unit_k)
        + mm_once(key_products_grad, unit_k, TN)
    )
    q_grad = scaling * inv_q * (unit_q_grad - raw_q * (inv_q * inv_q * row_sum(unit_q_grad * raw_q)))
    k_grad = inv_k * (unit_k_grad - raw_k * (inv_k * inv_k * row_sum(unit_k_grad * raw_k)))
    for h in range(heads):
        cols = slice(h * depth, (h + 1) * depth)
        own = slice(h * rows, (h + 1) * rows)
        gdq_out[:, cols] = q_grad[own].astype(BF16)
        gdk_out[:, cols] = k_grad[own].astype(BF16)
        gdv_out[:, cols] = value_grad[own].astype(BF16)
    beta_grad = row_sum(solved_grad * remainder) + row_sum(lower_grad * faded_keys)
    exponent = faded_grad * query_products + key_products_grad * key_products
    tail_grad = row_sum(unit_k * fresh_back)
    growth_grad = row_sum(out_grad * query_reads) - row_sum(value_grad * key_reads)
    summed_grad = (
        row_sum(exponent) - to_column(column_sum(exponent)) - tail_grad + growth * growth_grad
    )
    end_grad = end_growth * by_parts(
        lambda h, b: jnp.broadcast_to(
            column_sum(row_sum(later[h, b] * states_ref[b, h])), (BLOCK, 1)
        )
    )
    decay_grad = (
        column_sum(jnp.where(causal, summed_grad, 0.0))
        + column_sum(jnp.where(same, tail_grad, 0.0))
        + to_row(end_grad)
    )
    beta_row = to_row(beta_grad)
    for h in range(heads):
        own = slice(h * rows, (h + 1) * rows)
        gdecay_out[h : h + 1, :] = decay_grad[:, own]
        gbeta_out[h : h + 1, :] = beta_row[:, own]

    attend(
        [j for j in range(1, min(reach, n - 1) + 1) if j % size],
        lambda j: (me >= j) & (rank < j),
        lambda j: (me + j < n) & (rank + j >= size),
    )

    dq_out[...] = (dq_acc[...] * scaling).astype(BF16)
    both_grads = jnp.concatenate(
        [(dkv_acc[:, :columns] * scaling).astype(BF16), dkv_acc[:, columns:].astype(BF16)], axis=1
    )
    w_all[me] = w_ref[...]
    for i in range(1, size):
        each(w_passes(i), "wait_recv")
    out_rows = dx_out.shape[0]
    pieces_each = out_rows // w_rows

    def dx_rows(owner):
        piece = w_all[pl.ds(owner * pieces_each, pieces_each)].reshape(out_rows, 2 * columns)
        return dot(piece, both_grads, NT)

    def dx_copy(j):
        return pltpu.make_async_remote_copy(
            src_ref=dx_send.at[j - 1],
            dst_ref=dx_recv.at[j - 1],
            send_sem=x_send.at[j - 1],
            recv_sem=x_recv.at[j - 1],
            device_id={"head": lax.rem(my_head + j, head_n)},
            device_id_type=MESH,
        )

    for j in range(1, head_n):
        dx_send[j - 1] = dx_rows(lax.rem(my_head + j, head_n))
        dx_copy(j).start()
    result = dx_rows(my_head)
    for j in range(1, head_n):
        dx_copy(j).wait_recv()
        result = result + dx_recv[j - 1]
    dx_out[...] = result.astype(BF16)

    own_copies("wait_send")
    for m in range(1, hops + 1):
        pass_keys(m, "wait_send")
        pass_queries(m, "wait_send")
    for m in range(1, groups):
        w_copy(m).wait_send()
    for i in range(1, size):
        each(w_passes(i), "wait_send")
    for j in range(1, size):
        ab_copy(j).wait_send()
    if groups > 1:
        @pl.when(group > 0)
        def _():
            carry_copy().wait_send()

    for j in range(1, head_n):
        dx_copy(j).wait_send()


def hand_over(*refs):
    half = len(refs) // 2
    for source, target in zip(refs[:half], refs[half:]):
        target[...] = source[...]


def per_device(n, head_n, *args):
    attn_q, attn_lse, w_kv, states = args[0], args[5], args[6], args[13]
    rows, columns = attn_q.shape
    heads = attn_lse.shape[0]
    depth = columns // heads
    reach = min(WINDOW // rows, n - 1)
    size = group_size(n, WINDOW // rows)
    blocks = states.shape[0]
    groups = n // size
    hops = max(min(reach // size, groups - 1), 1)
    w_rows = w_kv.shape[0]
    out_rows = n * w_rows // head_n
    args = list(args)
    args[6] = w_kv.reshape(w_rows, 2 * columns)
    dma = pltpu.SemaphoreType.DMA
    vmem = pl.BlockSpec(memory_space=pltpu.VMEM)
    others = max(head_n - 1, 1)
    results = pl.pallas_call(
        functools.partial(kernel, n, head_n),
        out_shape=(
            jax.ShapeDtypeStruct((rows, columns), BF16),
            jax.ShapeDtypeStruct((out_rows, rows), BF16),
            jax.ShapeDtypeStruct((rows, columns), BF16),
            jax.ShapeDtypeStruct((rows, columns), BF16),
            jax.ShapeDtypeStruct((rows, columns), BF16),
            jax.ShapeDtypeStruct((heads, rows), F32),
            jax.ShapeDtypeStruct((heads, rows), F32),
        ),
        in_specs=[vmem] * len(args),
        out_specs=(vmem,) * 7,
        scratch_shapes=[
            pltpu.VMEM((reach, 2, rows, columns), BF16),
            pltpu.VMEM((reach, 2, rows, columns), BF16),
            pltpu.VMEM((2 * heads, rows), F32),
            pltpu.VMEM((reach, 2 * heads, rows), F32),
            pltpu.VMEM((n, w_rows, 2 * columns), BF16),
            pltpu.VMEM((size, heads, depth, 2 * depth), BF16),
            pltpu.VMEM((heads, depth, depth), BF16),
            pltpu.VMEM((heads, depth, depth), BF16),
            pltpu.VMEM((others, out_rows, rows), F32),
            pltpu.VMEM((others, out_rows, rows), F32),
            pltpu.VMEM((rows, columns), F32),
            pltpu.VMEM((rows, 2 * columns), F32),
            pltpu.VMEM((heads, blocks, depth, 2 * depth), F32),
            dma((reach, 2)), dma((reach, 2)),
            dma((reach, 2)), dma((reach, 2)),
            dma((reach,)), dma((reach,)),
            dma((groups,)), dma((size, groups)),
            dma((hops, size, 2)), dma((hops, size, 2)), dma((hops, size)), dma((size, groups)),
            dma((size,)), dma((size,)),
            dma, dma,
            dma((others,)), dma((others,)),
        ],
        compiler_params=pltpu.CompilerParams(
            collective_id=0, has_side_effects=True, vmem_limit_bytes=60000000
        ),
        name="layer_backward",
    )(*args)
    return pl.pallas_call(
        hand_over,
        out_shape=[jax.ShapeDtypeStruct(item.shape, item.dtype) for item in results],
        in_specs=[vmem] * len(results),
        out_specs=[vmem] * len(results),
        name="hand_over",
    )(*results)


def solution(mesh):
    rows = P("seq", "head")
    gates = P("head", "seq")
    return jax.shard_map(
        functools.partial(per_device, mesh.shape["seq"], mesh.shape["head"]),
        mesh=mesh,
        in_specs=(
            rows, rows, rows, rows, rows, gates, P("seq", None, "head"),
            rows, rows, rows, rows, gates, gates, P("seq", "head", None, None),
        ),
        out_specs=(rows, gates, rows, rows, rows, gates, gates),
        check_vma=False,
    )
```
